128 devices in a mesh: gx: 4 (over y), gy: 4 (over x), gz: 8 (over z, core).
Axes of the slice: x: 4, y: 4, z: 4, core: 2. Of those that a mesh axis runs over, the one named last changes fastest.
Arguments:
- blocks: bfloat16 [32768, 64, 448], P(('gx', 'gy', 'gz')), may hold values from -1.1953125 to 1.1953125
- prolong: bfloat16 [32768, 4096], P(('gx', 'gy', 'gz')), may hold values from -0.75 to 0.75
- new_owner: int32 [32768], P(('gx', 'gy', 'gz')), may hold values from 0 to 127, as said below
- arrival: int32 [32768], P(('gx', 'gy', 'gz')), may hold values from 0 to 303, as said below
- columns: int32 [32768, 7], P(('gx', 'gy', 'gz')), may hold values from -1 to 639, as said below
- targets: int32 [32768, 7], P(('gx', 'gy', 'gz')), may hold values from 0 to 223, as said below
- ghost_lists: int32 [128, 6, 64], P(('gx', 'gy', 'gz')), may hold values from 0 to 255
- touched: int32 [128, 224], P(('gx', 'gy', 'gz')), may hold values from 0 to 63
Outputs:
- coarse: float32 [8192, 4096], P(('gx', 'gy', 'gz'))
The draws below stay inside these ranges and needn't reach their ends.
Inputs may be any that keep to these rules, and one draw needn't show every extreme that they name: `new_owner`: every row's new owner is in the same gz column (same gx and gy index); two devices adjacent along gz swap the same number of rows both ways, between 4 and 6, and some adjacent pair swaps exactly 6; every other pair of distinct devices of a column swaps exactly 2 rows each way; so every device holds 256 rows after the move. `arrival`: below 256: an old row of the same device that stays; else 256 + p * 6 + r, the row of rank r among those that the device of gz index p of the column hands over; every staying and every handed-over row is named once. `columns`: entry 0 is the row's own new local index; entry k >= 1 is -1, a local row below 256, or 256 + (k - 1) * 64 + q, the q-th block sent by the neighbour in direction k - 1, which then exists. `targets`: a value v * 32 + q names, for v = 0, a coarse block of the device itself, and for v >= 1 one owned by its neighbour in direction v - 1, which then exists.
All inputs are finite; a program needn't handle non-finite values.
Results may differ from the reference program's by a relative error of at most 0.0029.
Values may be sent and summed in bfloat16 or wider, within the bound.
No kernel may reach another device: no remote copies, remote signals or barrier semaphores. Data moves between devices by JAX's collectives and lax.ppermute only.
A program may use at most 256 MiB of HBM per device.

```python
import jax
import jax.numpy as jnp
from jax import lax

B = 64
NBR = 7
ROWS_DEV = 256
ROWS = 32768
FAR = 2
CAP = 6
GCAP = 64
UCAP = 32
U_DEV = 224
CE_DEV = 64
CE = 8192
N_GX = 4
N_GY = 4
N_GZ = 8
DEVICES = 128


def neighbour_table_drawn():
    device_count = ROWS // ROWS_DEV
    device_ids = jnp.arange(device_count, dtype=jnp.int32)
    coords = [device_ids // (N_GY * N_GZ), device_ids // N_GZ % N_GY, device_ids % N_GZ]
    extents = [N_GX, N_GY, N_GZ]
    strides = [N_GY * N_GZ, N_GZ, 1]
    listed = []
    for facing in range(6):
        axis_pos = facing // 2
        orient = 1 - 2 * (facing % 2)
        shifted = coords[axis_pos] + orient
        inside = (shifted >= 0) & (shifted < extents[axis_pos])
        listed.append(jnp.where(inside, device_ids + orient * strides[axis_pos], -1))
    return jnp.stack(listed, axis=1).astype(jnp.int32)


def repartition_plan(key):
    device_count = ROWS // ROWS_DEV
    column_count = device_count // N_GZ
    key_counts, key_order, key_shuffle = jax.random.split(key, 3)
    near_counts = jax.random.randint(key_counts, (column_count, N_GZ - 1), 2 * FAR, CAP + 1)
    near_counts = near_counts.at[0, N_GZ - 2].set(CAP)
    layer_ids = jnp.arange(N_GZ, dtype=jnp.int32)
    layer_gap = layer_ids[:, None] - layer_ids[None, :]
    lower_layer = jnp.minimum(jnp.minimum(layer_ids[:, None], layer_ids[None, :]), N_GZ - 2)
    counts = jnp.where(jnp.abs(layer_gap)[None] == 1, near_counts[:, lower_layer], jnp.where(layer_gap[None] != 0, FAR, 0)).astype(jnp.int32)
    out_counts = counts.reshape(device_count, N_GZ)
    in_counts = jnp.transpose(counts, (0, 2, 1)).reshape(device_count, N_GZ)
    cumulative = jnp.cumsum(out_counts, axis=1)
    orders = jax.vmap(lambda subkey: jax.random.permutation(subkey, ROWS_DEV))(jax.random.split(key_order, device_count)).astype(jnp.int32)
    positions = jnp.arange(ROWS_DEV, dtype=jnp.int32)
    peer_at = jnp.sum((positions[None, :, None] >= cumulative[:, None, :]).astype(jnp.int32), axis=2)
    device_ids = jnp.arange(device_count, dtype=jnp.int32)
    column_base = device_ids - device_ids % N_GZ
    owner_at = jnp.where(peer_at < N_GZ, column_base[:, None] + peer_at, device_ids[:, None]).astype(jnp.int32)
    owner_ids = jnp.zeros((device_count, ROWS_DEV), jnp.int32).at[device_ids[:, None], orders].set(owner_at)
    kept_rows = owner_ids == device_ids[:, None]
    slot_rank = jnp.arange(CAP, dtype=jnp.int32)
    incoming = (slot_rank[None, None, :] < in_counts[:, :, None]).reshape(device_count, N_GZ * CAP)
    valid_slots = jnp.concatenate([kept_rows, incoming], axis=1)
    length = ROWS_DEV + N_GZ * CAP
    slot_codes = jnp.arange(length, dtype=jnp.int32)
    shuffled = jax.vmap(lambda subkey: jax.random.permutation(subkey, length))(jax.random.split(key_shuffle, device_count)).astype(jnp.int32)
    scores = jnp.where(valid_slots, shuffled, length + slot_codes[None, :])
    picked = jnp.argsort(scores, axis=1)[:, :ROWS_DEV].astype(jnp.int32)
    return (owner_ids.reshape(-1).astype(jnp.int32), picked.reshape(-1).astype(jnp.int32))


def draw_new_owner(key, part):
    owner_ids, picked = repartition_plan(jax.random.fold_in(key, 11))
    return owner_ids


def draw_arrival(key, part):
    owner_ids, picked = repartition_plan(jax.random.fold_in(key, 11))
    return picked


def draw_columns(key, part):
    neighbours = neighbour_table_drawn()
    key_kind, key_local, key_ghost = jax.random.split(jax.random.fold_in(key, 23), 3)
    row_ids = jnp.arange(ROWS, dtype=jnp.int32)
    own_index = (row_ids % ROWS_DEV)[:, None]
    kind_draw = jax.random.randint(key_kind, (ROWS, NBR - 1), 0, 20)
    local_rows = jax.random.randint(key_local, (ROWS, NBR - 1), 0, ROWS_DEV)
    ghost_slot = jax.random.randint(key_ghost, (ROWS, NBR - 1), 0, GCAP)
    facing = jnp.arange(NBR - 1, dtype=jnp.int32)[None, :]
    present = neighbours[row_ids // ROWS_DEV] >= 0
    ghost_index = ROWS_DEV + facing * GCAP + ghost_slot
    others = jnp.where(kind_draw == 0, -1, jnp.where(kind_draw < 8, jnp.where(present, ghost_index, -1), local_rows))
    lists = jnp.concatenate([own_index, others], axis=1).astype(jnp.int32)
    lists = lists.at[0, 1].set(-1)
    lists = lists.at[ROWS_DEV, NBR - 1].set(ROWS_DEV + 6 * GCAP - 1)
    return lists


def draw_targets(key, part):
    neighbours = neighbour_table_drawn()
    key_dir, key_slot = jax.random.split(jax.random.fold_in(key, 31))
    row_ids = jnp.arange(ROWS, dtype=jnp.int32)
    pick_draw = jax.random.randint(key_dir, (ROWS,), 0, 12)
    facing = jnp.clip(pick_draw - 6, 0, 5)
    present = neighbours[row_ids // ROWS_DEV] >= 0
    matches = jnp.arange(6, dtype=jnp.int32)[None, :] == facing[:, None]
    has_peer = jnp.sum((matches & present).astype(jnp.int32), axis=1) > 0
    direction = jnp.where((pick_draw >= 6) & has_peer, facing + 1, 0)
    slot_draw = jax.random.randint(key_slot, (ROWS, NBR), 0, UCAP)
    result = direction[:, None] * UCAP + slot_draw
    result = result.at[ROWS_DEV].set(6 * UCAP + slot_draw[ROWS_DEV])
    result = result.at[ROWS_DEV, 0].set(7 * UCAP - 1)
    result = result.at[0, 0].set(0)
    return result.astype(jnp.int32)


def set_ends(values, key, low, largest):
    extent = values.shape
    place = [jax.random.randint(jax.random.fold_in(key, axis), (), 0, extent[axis]) for axis in range(len(extent))]
    values = values.at[tuple(place)].set(low)
    longest = extent.index(max(extent))
    place[longest] = (place[longest] + 1) % extent[longest]
    return values.at[tuple(place)].set(largest)


def block_levels(key, shape, pieces, smallest, largest):
    def one(dim, blocks):
        heights = jax.random.uniform(jax.random.fold_in(jax.random.fold_in(key, 6), dim), (blocks,), jnp.float32, smallest / len(pieces), largest / len(pieces))
        return jnp.repeat(jnp.exp(heights), shape[dim] // blocks).reshape((-1,) + (1,) * (len(shape) - dim - 1))

    loudness = one(*pieces[0])
    for cut in pieces[1:]:
        loudness = loudness * one(*cut)
    return loudness


def normal_values(own_key, extent, scale, reach, cuts=(), kind=jnp.bfloat16):
    gain = block_levels(own_key, extent, cuts, -0.22, 0.18) if cuts else 1.0
    drawn = jax.random.normal(own_key, extent, jnp.float32) * scale * gain
    return jnp.minimum(jnp.maximum(drawn, -reach), reach).astype(kind)


def setup_inputs(seed: int = 0) -> dict:
    seeds = jax.random.split(jax.random.key(seed), 9)
    blocks = normal_values(seeds[0], (ROWS, B, NBR * B), 0.2, 1.1953125, ((0, 128),))
    prolong = normal_values(seeds[1], (ROWS, B * B), B ** -0.5, 0.75, ((0, 128),))
    new_owner = draw_new_owner(jax.random.fold_in(seeds[8], 71), 0)
    arrival = draw_arrival(jax.random.fold_in(seeds[8], 71), 0)
    columns = draw_columns(jax.random.fold_in(seeds[8], 71), 0)
    targets = draw_targets(jax.random.fold_in(seeds[8], 71), 0)
    ghost_lists = set_ends(jax.random.randint(seeds[6], (DEVICES, 6, GCAP), 0, ROWS_DEV), jax.random.fold_in(seeds[6], 1), 0, ROWS_DEV - 1).astype(jnp.int32)
    touched = set_ends(jax.random.randint(seeds[7], (DEVICES, U_DEV), 0, CE_DEV), jax.random.fold_in(seeds[7], 1), 0, CE_DEV - 1).astype(jnp.int32)
    return {"blocks": blocks, "prolong": prolong, "new_owner": new_owner, "arrival": arrival, "columns": columns, "targets": targets, "ghost_lists": ghost_lists, "touched": touched}


def rank_within(labels, label_count):
    onehot = (labels[:, None] == jnp.arange(label_count, dtype=jnp.int32)[None, :]).astype(jnp.int32)
    before = jnp.cumsum(onehot, axis=0) - onehot
    return jnp.sum(before * onehot, axis=1).astype(jnp.int32)


def neighbour_table(device_count):
    device_ids = jnp.arange(device_count, dtype=jnp.int32)
    coords = [device_ids // (N_GY * N_GZ), (device_ids // N_GZ) % N_GY, device_ids % N_GZ]
    extents = [N_GX, N_GY, N_GZ]
    strides = [N_GY * N_GZ, N_GZ, 1]
    listed = []
    for facing in range(6):
        axis_pos = facing // 2
        orient = 1 - 2 * (facing % 2)
        shifted = coords[axis_pos] + orient
        inside = (shifted >= 0) & (shifted < extents[axis_pos])
        listed.append(jnp.where(inside, device_ids + orient * strides[axis_pos], -1))
    return jnp.stack(listed, axis=1).astype(jnp.int32)


def reference(blocks, prolong, new_owner, arrival, columns, targets, ghost_lists, touched):
    device_count = ROWS // ROWS_DEV
    neighbours = neighbour_table(device_count)
    row_ids = jnp.arange(ROWS, dtype=jnp.int32)
    source = (row_ids // ROWS_DEV).astype(jnp.int32)
    source_layer = (source % N_GZ).astype(jnp.int32)
    peer_layer = (new_owner % N_GZ).astype(jnp.int32)
    row_ranks = jax.vmap(lambda labels: rank_within(labels, N_GZ))(peer_layer.reshape(device_count, ROWS_DEV)).reshape(-1)
    table_size = device_count * N_GZ * CAP
    moved_rows = new_owner != source
    slot_key = jnp.where(moved_rows, (new_owner * N_GZ + source_layer) * CAP + row_ranks, table_size).astype(jnp.int32)
    inverse = jnp.zeros((table_size + 1,), jnp.int32).at[slot_key].set(row_ids)
    offset = jnp.maximum(arrival - ROWS_DEV, 0).astype(jnp.int32)
    lookup = ((source * N_GZ + offset // CAP) * CAP + offset % CAP).astype(jnp.int32)
    anchor = jnp.where(arrival < ROWS_DEV, source * ROWS_DEV + arrival, inverse[lookup]).astype(jnp.int32)
    arrived = blocks[anchor].reshape(device_count, ROWS_DEV, B, NBR * B)
    opposite = jnp.bitwise_xor(jnp.arange(6, dtype=jnp.int32), 1)
    slot_dir = (jnp.arange(U_DEV, dtype=jnp.int32) // UCAP).astype(jnp.int32)

    def one_device(coarse, inputs):
        rows_here, prolong_here, columns_here, targets_here, partners, touched_here, device_id = inputs
        safe_partners = jnp.maximum(partners, 0).astype(jnp.int32)
        ghost_index = (safe_partners[:, None] * ROWS_DEV + ghost_lists[safe_partners, opposite]).astype(jnp.int32)
        ghost_rows = prolong[ghost_index.reshape(-1)].reshape(6, GCAP, B * B)
        ghost_rows = jnp.where((partners >= 0)[:, None, None], ghost_rows, jnp.zeros((), prolong.dtype))
        block_table = jnp.concatenate([prolong_here, ghost_rows.reshape(-1, B * B)], axis=0).reshape(-1, B, B)
        live_mask = (columns_here >= 0).astype(jnp.float32)
        neighbour = block_table[jnp.maximum(columns_here, 0).astype(jnp.int32)]
        own_block = prolong_here.reshape(ROWS_DEV, B, B).astype(jnp.float32)
        left = jnp.einsum("rba,rbx->rax", own_block, rows_here.astype(jnp.float32), precision=lax.Precision.HIGHEST).astype(jnp.bfloat16)
        left = lax.optimization_barrier(left)
        left = left.reshape(ROWS_DEV, B, NBR, B).astype(jnp.float32)
        partial_blocks = jnp.einsum("rakb,rkbc->rkac", left, neighbour.astype(jnp.float32), precision=lax.Precision.HIGHEST)
        partial_blocks = partial_blocks * live_mask[:, :, None, None]
        slot_sums = jnp.zeros((U_DEV, B * B), jnp.float32).at[targets_here.reshape(-1).astype(jnp.int32)].add(partial_blocks.reshape(-1, B * B))
        owner_ids = jnp.where(slot_dir == 0, device_id, partners[jnp.clip(slot_dir - 1, 0, 5)]).astype(jnp.int32)
        has_owner = owner_ids >= 0
        entries = jnp.where(has_owner, owner_ids * CE_DEV + touched_here, 0).astype(jnp.int32)
        slot_sums = slot_sums * has_owner[:, None].astype(jnp.float32)
        coarse = coarse.at[entries].add(slot_sums)
        return coarse, None

    inputs = (arrived, prolong.reshape(device_count, ROWS_DEV, B * B), columns.reshape(device_count, ROWS_DEV, NBR), targets.reshape(device_count, ROWS_DEV, NBR), neighbours, touched, jnp.arange(device_count, dtype=jnp.int32))
    coarse, unused = lax.scan(one_device, jnp.zeros((CE, B * B), jnp.float32), inputs)
    return coarse
```

```python
import functools

import jax
import jax.numpy as jnp
from jax import lax
from jax.experimental import pallas as pl
from jax.experimental.pallas import tpu as pltpu
from jax.sharding import PartitionSpec as P

B = 64
NBR = 7
CAP = 6
FAR = 2
NEAR = CAP - FAR
GCAP = 64
UCAP = 32
U_DEV = 224
CE_DEV = 64
ROWS = 256
LAYERS = 8
HALF = 32
LANES = 128
AXES = ("gx", "gy", "gz")
SENT = LAYERS * FAR + 2 * NEAR
SENT_PAD = 32
ROW_LEN = 3 * B + HALF
GHOST_LEN = GCAP * HALF
EXTRA = 16
TABLE = ROWS + 6 * GCAP
VMEM_LIMIT = 62 * 1024 * 1024
bf16 = jnp.bfloat16
f32 = jnp.float32


def lower_lanes(shape):
    return lax.broadcasted_iota(jnp.int32, shape, len(shape) - 1) < B


def swap_lanes(v):
    return jnp.concatenate([v[:, B:], v[:, :B]], axis=1)


def shifted(value, axis, by):
    devices = lax.axis_size(axis)
    pairs = [(i, i + by) for i in range(devices) if 0 <= i + by < devices]
    return lax.ppermute(value, axis, pairs)


def pack_kernel(lists, prolong, extra, halves, *rest):
    sends, work = rest[:6], rest[6]
    low = lower_lanes((16, LANES))

    def group(g, carry):
        rows = pl.ds(pl.multiple_of(g * 16, 16), 16)
        for s in range(16):
            near = prolong[rows, s * LANES : (s + 1) * LANES].astype(f32)
            far = prolong[rows, (s + 16) * LANES : (s + 17) * LANES].astype(f32)
            even = jnp.where(low, near, pltpu.roll(far, B, 1))
            odd = jnp.where(low, pltpu.roll(near, B, 1), far)
            work[pl.ds(2 * s, 16, stride=HALF), :] = even
            work[pl.ds(2 * s + 1, 16, stride=HALF), :] = odd
        for e in range(16):
            halves[pl.ds(pl.multiple_of((g * 16 + e) * HALF, HALF), HALF), :] = work[
                e * HALF : (e + 1) * HALF, :
            ].astype(bf16)
        return carry

    lax.fori_loop(0, ROWS // 16, group, 0)

    def pick(q, carry):
        for j in range(6):
            row = lists[j, q]
            sends[j][pl.ds(pl.multiple_of(q * HALF, HALF), HALF), :] = halves[
                pl.ds(pl.multiple_of(row * HALF, HALF), HALF), :
            ]
        return carry

    lax.fori_loop(0, GCAP, pick, 0, unroll=4)
    for j in range(6):
        sends[j][GHOST_LEN:, :] = extra[...]


def pack(lists, prolong, extra):
    return pl.pallas_call(
        pack_kernel,
        grid_spec=pltpu.PrefetchScalarGridSpec(
            num_scalar_prefetch=1,
            grid=(1,),
            in_specs=[
                pl.BlockSpec((ROWS, B * B), lambda i, s: (0, 0)),
                pl.BlockSpec((EXTRA, LANES), lambda i, s: (0, 0)),
            ],
            out_specs=[pl.BlockSpec((ROWS * HALF, LANES), lambda i, s: (0, 0))]
            + [pl.BlockSpec((GHOST_LEN + EXTRA, LANES), lambda i, s: (0, 0))] * 6,
            scratch_shapes=[pltpu.VMEM((16 * HALF, LANES), f32)],
        ),
        out_shape=[jax.ShapeDtypeStruct((ROWS * HALF, LANES), bf16)]
        + [jax.ShapeDtypeStruct((GHOST_LEN + EXTRA, LANES), bf16)] * 6,
        compiler_params=pltpu.CompilerParams(vmem_limit_bytes=VMEM_LIMIT),
        name="pack",
    )(lists, prolong, extra)


def to_halves(chunk):
    top, bottom = chunk[:HALF, :], chunk[HALF:, :]
    first = jnp.concatenate([top[:, :B], bottom[:, :B]], axis=1)
    second = jnp.concatenate([top[:, B:], bottom[:, B:]], axis=1)
    return first, second


def left_kernel(picks, blocks, halves, left, far, up, down, table, transposed):
    j = pl.program_id(0)
    total = ROWS + SENT_PAD
    eye = (
        lax.broadcasted_iota(jnp.int32, (B, B), 0) == lax.broadcasted_iota(jnp.int32, (B, B), 1)
    ).astype(bf16)

    @pl.when(j == 0)
    def _():
        def turn(i, carry):
            h = halves[pl.ds(pl.multiple_of(i * HALF, HALF), HALF), :]
            block = jnp.concatenate([h[:, :B], h[:, B:]], axis=0)
            transposed[i] = lax.dot_general(
                eye, block, (((1,), (1,)), ((), ())), preferred_element_type=f32
            ).astype(bf16)
            return carry

        lax.fori_loop(0, ROWS, turn, 0, unroll=8)

    def relay(a, carry):
        table[pl.ds(pl.multiple_of(a * total, 8), total), :] = lax.dot_general(
            picks[...], blocks[a], (((1,), (1,)), ((), ())), preferred_element_type=f32
        )
        return carry

    lax.fori_loop(0, B, relay, 0, unroll=2)

    def multiply(i, carry):
        rows = table[pl.ds(i, B, stride=total), :].astype(bf16)
        chunk = jnp.dot(transposed[i], rows, preferred_element_type=f32).astype(bf16)
        first, second = to_halves(chunk)
        left[0, i] = first
        left[1, i] = second
        return carry

    lax.fori_loop(0, ROWS, multiply, 0, unroll=8)

    def sent(r):
        return table[pl.ds(ROWS + r, B, stride=total), :].astype(bf16)

    for r in range(SENT):
        if r < LAYERS * FAR:
            out, base = far.at[r // FAR], (r % FAR) * ROW_LEN
        elif r < LAYERS * FAR + NEAR:
            out, base = up, (r - LAYERS * FAR) * ROW_LEN
        else:
            out, base = down, (r - LAYERS * FAR - NEAR) * ROW_LEN

        @pl.when(j < 3)
        def _():
            out[pl.ds(pl.multiple_of(base + j * B, HALF), B), :] = sent(r)

        @pl.when(j == 3)
        def _():
            out[base + 3 * B : base + ROW_LEN, :] = to_halves(sent(r))[0]


def make_left(picks, blocks, halves):
    whole = lambda shape: pl.BlockSpec(shape, lambda j: (0,) * len(shape))
    return pl.pallas_call(
        left_kernel,
        grid=(4,),
        in_specs=[
            whole((ROWS + SENT_PAD, ROWS)),
            pl.BlockSpec((B, LANES, ROWS), lambda j: (0, j, 0)),
            whole((ROWS * HALF, LANES)),
        ],
        out_specs=[
            pl.BlockSpec((2, ROWS, HALF, LANES), lambda j: (j, 0, 0, 0)),
            whole((LAYERS, FAR * ROW_LEN, LANES)),
            whole((NEAR * ROW_LEN, LANES)),
            whole((NEAR * ROW_LEN, LANES)),
        ],
        out_shape=[
            jax.ShapeDtypeStruct((NBR + 1, ROWS, HALF, LANES), bf16),
            jax.ShapeDtypeStruct((LAYERS, FAR * ROW_LEN, LANES), bf16),
            jax.ShapeDtypeStruct((NEAR * ROW_LEN, LANES), bf16),
            jax.ShapeDtypeStruct((NEAR * ROW_LEN, LANES), bf16),
        ],
        scratch_shapes=[
            pltpu.VMEM((B * (ROWS + SENT_PAD), LANES), f32),
            pltpu.VMEM((ROWS, B, B), bf16),
        ],
        compiler_params=pltpu.CompilerParams(
            vmem_limit_bytes=VMEM_LIMIT, dimension_semantics=("arbitrary",)
        ),
        name="left",
    )(picks, blocks, halves)


PARTS = 8


def sums_kernel(
    arrival, place, left_hbm, halves, g0, g1, g2, g3, g4, g5, far, up, down,
    own, s0, s1, s2, s3, s4, s5,
    left, packed, diagonal, even, odd, moved, left_sem, table_sem, moved_sem,
):
    ghosts = (g0, g1, g2, g3, g4, g5)
    sends = (s0, s1, s2, s3, s4, s5)
    layer = place[NBR, 0]
    part = ROWS // PARTS
    table_copies = [pltpu.make_async_copy(halves, packed.at[: ROWS * HALF, :], table_sem.at[0])]
    for j in range(6):
        first = (ROWS + j * GCAP) * HALF
        table_copies.append(
            pltpu.make_async_copy(
                ghosts[j].at[:GHOST_LEN, :],
                packed.at[first : first + GHOST_LEN, :],
                table_sem.at[1 + j],
            )
        )
    moved_copies = [
        pltpu.make_async_copy(far, moved.at[: LAYERS * FAR * ROW_LEN, :], moved_sem.at[0]),
        pltpu.make_async_copy(
            up,
            moved.at[LAYERS * FAR * ROW_LEN : (LAYERS * FAR + NEAR) * ROW_LEN, :],
            moved_sem.at[1],
        ),
        pltpu.make_async_copy(
            down, moved.at[(LAYERS * FAR + NEAR) * ROW_LEN :, :], moved_sem.at[2]
        ),
    ]
    left_copies = [
        pltpu.make_async_copy(
            left_hbm.at[:NBR, pl.ds(n * part, part)],
            left.at[:, pl.ds(n * part, part)],
            left_sem.at[n],
        )
        for n in range(PARTS)
    ]
    for copy in table_copies + moved_copies + left_copies:
        copy.start()

    def clear(u, carry):
        even[u] = jnp.zeros((HALF, LANES), f32)
        odd[u] = jnp.zeros((HALF, LANES), f32)
        return carry

    lax.fori_loop(0, U_DEV + 1, clear, 0, unroll=5)

    low = lower_lanes((HALF, LANES)).astype(f32).astype(bf16)
    high = (1 - lower_lanes((HALF, LANES)).astype(jnp.int32)).astype(f32).astype(bf16)

    def expand(c, carry):
        h = packed[pl.ds(pl.multiple_of(c * HALF, HALF), HALF), :]
        turned = swap_lanes(h)
        diagonal[c, 0:HALF, :] = h * low
        diagonal[c, HALF:B, :] = turned * low
        diagonal[c, B : B + HALF, :] = turned * high
        diagonal[c, B + HALF :, :] = h * high
        return carry

    table_copies[0].wait()
    lax.fori_loop(0, ROWS, expand, 0, unroll=4)
    for j in range(6):
        table_copies[1 + j].wait()
    lax.fori_loop(ROWS, TABLE, expand, 0, unroll=4)
    for copy in moved_copies + left_copies:
        copy.wait()

    def arrive(i, carry):
        code = arrival[i]

        @pl.when(code >= ROWS)
        def _():
            source = (code - ROWS) // CAP
            rank = (code - ROWS) % CAP
            near = jnp.where(source < layer, LAYERS * FAR, LAYERS * FAR + NEAR) + rank - FAR
            slot = jnp.where(rank < FAR, source * FAR + rank, near)
            base = pl.multiple_of(slot * ROW_LEN, HALF)
            block = diagonal[i, 0:B, 0:B]
            for j in range(4):
                if j < 3:
                    rows = moved[pl.ds(base + j * B, B), :]
                else:
                    h = moved[pl.ds(base + 3 * B, HALF), :]
                    rows = jnp.concatenate([h, swap_lanes(h)], axis=0)
                chunk = lax.dot_general(
                    block, rows, (((0,), (0,)), ((), ())), preferred_element_type=f32
                ).astype(bf16)
                first, second = to_halves(chunk)
                left[2 * j, i] = first
                if j < 3:
                    left[2 * j + 1, i] = second

        return carry

    lax.fori_loop(0, ROWS, arrive, 0)

    def products(n, carry):
        for r in range(4):
            i = n * 4 + r
            for k in range(NBR):
                code = place[k, i]
                u, c = code % 256, code // 256
                total = even if (k + r * NBR) % 2 == 0 else odd
                total[u] += jnp.dot(left[k, i], diagonal[c], preferred_element_type=f32)
        return carry

    lax.fori_loop(0, ROWS // 4, products, 0)
    own[...] = even[:UCAP] + odd[:UCAP]
    for j in range(6):
        first = (j + 1) * UCAP
        sends[j][...] = (even[first : first + UCAP] + odd[first : first + UCAP]).astype(bf16)


def make_sums(arrival, place, left, halves, ghosts, far, up, down):
    hbm = pl.BlockSpec(memory_space=pl.ANY)
    block = pl.BlockSpec((UCAP, HALF, LANES), lambda i, *s: (0, 0, 0))
    return pl.pallas_call(
        sums_kernel,
        grid_spec=pltpu.PrefetchScalarGridSpec(
            num_scalar_prefetch=2,
            grid=(1,),
            in_specs=[hbm] * 11,
            out_specs=[block] * 7,
            scratch_shapes=[
                pltpu.VMEM((NBR, ROWS, HALF, LANES), bf16),
                pltpu.VMEM((TABLE * HALF, LANES), bf16),
                pltpu.VMEM((TABLE, LANES, LANES), bf16),
                pltpu.VMEM((U_DEV + 1, HALF, LANES), f32),
                pltpu.VMEM((U_DEV + 1, HALF, LANES), f32),
                pltpu.VMEM((SENT * ROW_LEN, LANES), bf16),
                pltpu.SemaphoreType.DMA((PARTS,)),
                pltpu.SemaphoreType.DMA((7,)),
                pltpu.SemaphoreType.DMA((3,)),
            ],
        ),
        out_shape=[jax.ShapeDtypeStruct((UCAP, HALF, LANES), f32)]
        + [jax.ShapeDtypeStruct((UCAP, HALF, LANES), bf16)] * 6,
        compiler_params=pltpu.CompilerParams(vmem_limit_bytes=VMEM_LIMIT),
        name="sums",
    )(arrival, place, left, halves, *ghosts, far, up, down)


def final_kernel(numbers, own, r0, r1, r2, r3, r4, r5, out, total):
    parts = (own, r0, r1, r2, r3, r4, r5)
    total[...] = jnp.zeros_like(total)

    def add(q, carry):
        for v in range(7):
            rows = pl.ds(pl.multiple_of(numbers[v, q] * HALF, HALF), HALF)
            total[rows, :] += parts[v][q].astype(f32)
        return carry

    lax.fori_loop(0, UCAP, add, 0, unroll=2)
    low = lower_lanes((8, LANES))

    for g in range(CE_DEV // 8):
        for s in range(16):
            a = total[pl.ds(g * 8 * HALF + 2 * s, 8, stride=HALF), :]
            b = total[pl.ds(g * 8 * HALF + 2 * s + 1, 8, stride=HALF), :]
            out[g * 8 : g * 8 + 8, s * LANES : (s + 1) * LANES] = jnp.where(
                low, a, pltpu.roll(b, B, 1)
            )
            out[g * 8 : g * 8 + 8, (s + 16) * LANES : (s + 17) * LANES] = jnp.where(
                low, pltpu.roll(a, B, 1), b
            )


def make_final(numbers, parts):
    block = pl.BlockSpec((UCAP, HALF, LANES), lambda i, *s: (0, 0, 0))
    return pl.pallas_call(
        final_kernel,
        grid_spec=pltpu.PrefetchScalarGridSpec(
            num_scalar_prefetch=1,
            grid=(1,),
            in_specs=[block] * 7,
            out_specs=pl.BlockSpec((CE_DEV, B * B), lambda i, *s: (0, 0)),
            scratch_shapes=[pltpu.VMEM((CE_DEV * HALF, LANES), f32)],
        ),
        out_shape=jax.ShapeDtypeStruct((CE_DEV, B * B), f32),
        compiler_params=pltpu.CompilerParams(vmem_limit_bytes=VMEM_LIMIT),
        name="final",
    )(numbers, *parts)


def neighbour_shift(value, facing):
    axis = AXES[facing // 2]
    return shifted(value, axis, 1 - 2 * (facing % 2))


def shards(blocks, prolong, new_owner, arrival, columns, targets, ghost_lists, touched):
    own_layer = lax.axis_index("gz")
    touched_here = touched[0]

    extra = jnp.pad(touched_here, (0, EXTRA * LANES - U_DEV)).reshape(EXTRA, LANES).astype(bf16)
    halves, *outbound = pack(ghost_lists[0], prolong, extra)
    ghosts = [neighbour_shift(outbound[facing ^ 1], facing ^ 1) for facing in range(6)]

    peer = new_owner % LAYERS
    labels = jnp.arange(LAYERS, dtype=jnp.int32)
    onehot = peer[:, None] == labels[None, :]
    earlier = jnp.arange(ROWS)[None, :] < jnp.arange(ROWS)[:, None]
    same = peer[:, None] == peer[None, :]
    rank = jnp.sum((earlier & same).astype(jnp.int32), axis=1)
    near = jnp.where(peer > own_layer, LAYERS * FAR, LAYERS * FAR + NEAR) + rank - FAR
    slot = jnp.where(rank < FAR, peer * FAR + rank, near)
    slot = jnp.where(peer == own_layer, -1, slot)
    old = jnp.arange(ROWS, dtype=jnp.int32)
    picks = jnp.concatenate(
        [
            arrival[:, None] == old[None, :],
            jnp.arange(SENT_PAD, dtype=jnp.int32)[:, None] == slot[None, :],
        ],
        axis=0,
    ).astype(bf16)

    left, far, up, down = make_left(picks, jnp.transpose(blocks, (1, 2, 0)), halves)
    far_in = lax.all_to_all(far, "gz", split_axis=0, concat_axis=0, tiled=True)
    up_in = shifted(up, "gz", 1)
    down_in = shifted(down, "gz", -1)

    cols = columns.T
    place = jnp.where(cols >= 0, cols * 256 + targets.T, U_DEV)
    place = jnp.concatenate([place, jnp.full((1, ROWS), own_layer, jnp.int32)], axis=0)
    own, *sends = make_sums(
        arrival, place, left, halves, ghosts,
        far_in.reshape(LAYERS * FAR * ROW_LEN, LANES), up_in, down_in,
    )
    got = [neighbour_shift(sends[facing], facing) for facing in range(6)]

    numbers = [touched_here[:UCAP]]
    for facing in range(6):
        flat = ghosts[facing ^ 1][GHOST_LEN : GHOST_LEN + 2].reshape(-1)
        first = (facing + 1) * UCAP
        numbers.append(flat[first : first + UCAP].astype(jnp.int32))
    return make_final(jnp.stack(numbers), [own] + got)


def solution(mesh):
    return jax.shard_map(
        shards,
        mesh=mesh,
        in_specs=(
            P(AXES, None, None),
            P(AXES, None),
            P(AXES),
            P(AXES),
            P(AXES, None),
            P(AXES, None),
            P(AXES, None, None),
            P(AXES, None),
        ),
        out_specs=P(AXES, None),
        check_vma=False,
    )
```

```python
import jax
import jax.numpy as jnp
from jax import lax
from jax.experimental import pallas as pl
from jax.experimental.pallas import tpu as pltpu
from jax.sharding import PartitionSpec as P


B = 64
NBR = 7
CAP = 6
FAR = 2
NEAR = CAP - FAR
GCAP = 64
UCAP = 32
U_DEV = 224
CE_DEV = 64
ROWS = 256
LAYERS = 8
HALF = 32
LANES = 128
AXES = ("gx", "gy", "gz")
SENT = LAYERS * FAR + 2 * NEAR
SENT_PAD = 32
ROW_LEN = 3 * B + HALF
GHOST_LEN = GCAP * HALF
EXTRA = 16
TABLE = ROWS + 6 * GCAP
VMEM_LIMIT = 62 * 1024 * 1024
PITCH = HALF + 1
bf16 = jnp.bfloat16
f32 = jnp.float32


def lower_lanes(shape):
    return lax.broadcasted_iota(jnp.int32, shape, len(shape) - 1) < B


def swap_lanes(v):
    return jnp.concatenate([v[:, B:], v[:, :B]], axis=1)


def shifted(value, axis, by):
    devices = lax.axis_size(axis)
    pairs = [(i, i + by) for i in range(devices) if 0 <= i + by < devices]
    return lax.ppermute(value, axis, pairs)


def pack_kernel(lists, prolong, extra, halves, *rest):
    sends, work = rest[:6], rest[6]
    low = lower_lanes((16, LANES))

    def group(g, carry):
        rows = pl.ds(pl.multiple_of(g * 16, 16), 16)
        for s in range(16):
            near = prolong[rows, s * LANES : (s + 1) * LANES].astype(f32)
            far = prolong[rows, (s + 16) * LANES : (s + 17) * LANES].astype(f32)
            even = jnp.where(low, near, pltpu.roll(far, B, 1))
            odd = jnp.where(low, pltpu.roll(near, B, 1), far)
            work[pl.ds(2 * s, 16, stride=PITCH), :] = even
            work[pl.ds(2 * s + 1, 16, stride=PITCH), :] = odd
        for e in range(16):
            halves[pl.ds(pl.multiple_of((g * 16 + e) * HALF, HALF), HALF), :] = work[
                e * PITCH : e * PITCH + HALF, :
            ].astype(bf16)
        return carry

    lax.fori_loop(0, ROWS // 16, group, 0)

    def pick(q, carry):
        for j in range(6):
            row = lists[j, q]
            sends[j][pl.ds(pl.multiple_of(q * HALF, HALF), HALF), :] = halves[
                pl.ds(pl.multiple_of(row * HALF, HALF), HALF), :
            ]
        return carry

    lax.fori_loop(0, GCAP, pick, 0, unroll=4)
    for j in range(6):
        sends[j][GHOST_LEN:, :] = extra[...]


def pack(lists, prolong, extra):
    return pl.pallas_call(
        pack_kernel,
        grid_spec=pltpu.PrefetchScalarGridSpec(
            num_scalar_prefetch=1,
            grid=(1,),
            in_specs=[
                pl.BlockSpec((ROWS, B * B), lambda i, s: (0, 0)),
                pl.BlockSpec((EXTRA, LANES), lambda i, s: (0, 0)),
            ],
            out_specs=[pl.BlockSpec((ROWS * HALF, LANES), lambda i, s: (0, 0))]
            + [pl.BlockSpec((GHOST_LEN + EXTRA, LANES), lambda i, s: (0, 0))] * 6,
            scratch_shapes=[pltpu.VMEM((16 * PITCH, LANES), f32)],
        ),
        out_shape=[jax.ShapeDtypeStruct((ROWS * HALF, LANES), bf16)]
        + [jax.ShapeDtypeStruct((GHOST_LEN + EXTRA, LANES), bf16)] * 6,
        compiler_params=pltpu.CompilerParams(vmem_limit_bytes=VMEM_LIMIT),
        cost_estimate=pl.CostEstimate(flops=0, transcendentals=0, bytes_accessed=8_000_000),
        name="pack",
    )(lists, prolong, extra)


STEPS = 4
A_STEP = B // STEPS
R_STEP = ROWS // STEPS
TOTAL = ROWS + SENT_PAD
SPAN = TOTAL + 1


def left_kernel(
    layer, labels, blocks, halves, left, far, up, down, table0, table1, transposed, picks
):
    j, step = pl.program_id(0), pl.program_id(1)
    tables = (table0, table1)
    square = (ROWS, ROWS)

    @pl.when((j == 0) & (step == 0))
    def _():
        eye = (
            lax.broadcasted_iota(jnp.int32, (B, B), 0)
            == lax.broadcasted_iota(jnp.int32, (B, B), 1)
        ).astype(bf16)

        low = lower_lanes((B, LANES))

        def turn(n, carry):
            tiles = []
            for q in range(4):
                h = halves[pl.ds(pl.multiple_of((n * 4 + q) * HALF, HALF), HALF), :]
                tiles += [h[:, :B], h[:, B:]]
            got = lax.dot_general(
                eye,
                jnp.concatenate(tiles, axis=0),
                (((1,), (1,)), ((), ())),
                preferred_element_type=f32,
            )
            for q in range(4):
                pair = got[:, (q // 2) * LANES : (q // 2 + 1) * LANES]
                mine = low if q % 2 == 0 else jnp.logical_not(low)
                transposed[n * 4 + q] = jnp.where(mine, pair, 0.0).astype(bf16)
            return carry

        lax.fori_loop(0, ROWS // 4, turn, 0, unroll=8)

        arrival, owner = labels[0:1, :], labels[1:2, :]
        down_rows = lax.broadcasted_iota(jnp.int32, square, 0)
        along = lax.broadcasted_iota(jnp.int32, square, 1)
        taken = (down_rows == arrival).astype(f32).astype(bf16)
        unit = (down_rows == along).astype(f32).astype(bf16)
        picks[:ROWS, :] = lax.dot_general(
            unit, taken, (((1,), (1,)), ((), ())), preferred_element_type=f32
        ).astype(bf16)
        peer = lax.rem(owner, LAYERS)
        member = lax.broadcasted_iota(jnp.int32, (16, ROWS), 0) == peer
        earlier = (down_rows < along).astype(f32).astype(bf16)
        before = jnp.dot(
            member.astype(f32).astype(bf16), earlier, preferred_element_type=f32
        )
        rank = jnp.sum(jnp.where(member, before, 0.0), axis=0, keepdims=True).astype(jnp.int32)
        near = jnp.where(peer > layer[0], LAYERS * FAR, LAYERS * FAR + NEAR) + rank - FAR
        slot = jnp.where(rank < FAR, peer * FAR + rank, near)
        slot = jnp.where(peer == layer[0], -1, slot)
        sent = lax.broadcasted_iota(jnp.int32, (SENT_PAD, ROWS), 0) == slot
        picks[ROWS:, :] = sent.astype(f32).astype(bf16)

    @pl.when(step < STEPS)
    def _():
        def relay(n, carry):
            rows = pl.ds((step * A_STEP + n) * SPAN, TOTAL)
            got = lax.dot_general(
                picks[...], blocks[n], (((1,), (1,)), ((), ())), preferred_element_type=f32
            )
            table0[rows, :] = got[:, :LANES]
            table1[rows, :] = got[:, LANES:]
            return carry

        lax.fori_loop(0, A_STEP, relay, 0, unroll=8)

    @pl.when(step >= STEPS)
    def _():
        keep = lower_lanes((B, LANES)) | (j == 0)

        def multiply(n, carry):
            i = (step - STEPS) * R_STEP + 2 * n
            rows = [
                jnp.concatenate(
                    [t[pl.ds(i + q, B, stride=SPAN), :].astype(bf16) for t in tables], axis=1
                )
                for q in range(2)
            ]
            pairs = jnp.concatenate([transposed[i], transposed[i + 1]], axis=0)
            got = jnp.dot(pairs, jnp.concatenate(rows, axis=0), preferred_element_type=f32)
            for q in range(2):
                part = got[q * B : (q + 1) * B]
                left[0, 2 * n + q] = part[:, :LANES].astype(bf16)
                left[1, 2 * n + q] = jnp.where(keep, part[:, LANES:], 0.0).astype(bf16)
            return carry

        lax.fori_loop(0, R_STEP // 2, multiply, 0, unroll=16)

    def place_of(r):
        if r < LAYERS * FAR:
            return far.at[r // FAR], (r % FAR) * ROW_LEN
        if r < LAYERS * FAR + NEAR:
            return up, (r - LAYERS * FAR) * ROW_LEN
        return down, (r - LAYERS * FAR - NEAR) * ROW_LEN

    @pl.when((step == STEPS) & (j == 0))
    def _():
        for r in range(SENT):
            out, base = place_of(r)
            for c in range(2):
                out[base + c * B : base + (c + 1) * B, :] = tables[c][
                    pl.ds(ROWS + r, B, stride=SPAN), :
                ].astype(bf16)

    @pl.when((step == STEPS) & (j == 1))
    def _():
        for r in range(SENT):
            out, base = place_of(r)
            out[base + 2 * B : base + 3 * B, :] = table0[
                pl.ds(ROWS + r, B, stride=SPAN), :
            ].astype(bf16)
            last = table1[pl.ds(ROWS + r, B, stride=SPAN), :].astype(bf16)
            out[base + 3 * B : base + ROW_LEN, :] = jnp.concatenate(
                [last[:HALF, :B], last[HALF:, :B]], axis=1
            )


def make_left(layer, labels, blocks, halves):
    whole = lambda shape: pl.BlockSpec(shape, lambda j, s, layer: (0,) * len(shape))
    return pl.pallas_call(
        left_kernel,
        grid_spec=pltpu.PrefetchScalarGridSpec(
            num_scalar_prefetch=1,
            grid=(2, 2 * STEPS),
            in_specs=[
                whole((2, ROWS)),
                pl.BlockSpec(
                    (A_STEP, 2 * LANES, ROWS),
                    lambda j, s, layer: (jnp.minimum(s, STEPS - 1), j, 0),
                ),
                whole((ROWS * HALF, LANES)),
            ],
            out_specs=[
                pl.BlockSpec(
                    (2, R_STEP, B, LANES),
                    lambda j, s, layer: (j, jnp.maximum(s - STEPS, 0), 0, 0),
                ),
                whole((LAYERS, FAR * ROW_LEN, LANES)),
                whole((NEAR * ROW_LEN, LANES)),
                whole((NEAR * ROW_LEN, LANES)),
            ],
            scratch_shapes=[
                pltpu.VMEM((B * SPAN, LANES), f32),
                pltpu.VMEM((B * SPAN, LANES), f32),
                pltpu.VMEM((ROWS, B, LANES), bf16),
                pltpu.VMEM((TOTAL, ROWS), bf16),
            ],
        ),
        out_shape=[
            jax.ShapeDtypeStruct((4, ROWS, B, LANES), bf16),
            jax.ShapeDtypeStruct((LAYERS, FAR * ROW_LEN, LANES), bf16),
            jax.ShapeDtypeStruct((NEAR * ROW_LEN, LANES), bf16),
            jax.ShapeDtypeStruct((NEAR * ROW_LEN, LANES), bf16),
        ],
        compiler_params=pltpu.CompilerParams(
            vmem_limit_bytes=VMEM_LIMIT, dimension_semantics=("arbitrary", "arbitrary")
        ),
        cost_estimate=pl.CostEstimate(
            flops=12_000_000_000, transcendentals=0, bytes_accessed=60_000_000
        ),
        name="left",
    )(layer, labels, blocks, halves)


PARTS = 8
UNROLL = 8


def sums_kernel(
    moved_rows, place, left_hbm, halves, g0, g1, g2, g3, g4, g5, far, up, down,
    own, s0, s1, s2, s3, s4, s5,
    left, packed, double, acc0, acc1, moved, left_sem, table_sem, moved_sem,
):
    ghosts = (g0, g1, g2, g3, g4, g5)
    sends = (s0, s1, s2, s3, s4, s5)
    totals = (acc0, acc1)
    part = ROWS // PARTS
    table_copies = [pltpu.make_async_copy(halves, packed.at[: ROWS * HALF, :], table_sem.at[0])]
    for j in range(6):
        first = (ROWS + j * GCAP) * HALF
        table_copies.append(
            pltpu.make_async_copy(
                ghosts[j].at[:GHOST_LEN, :],
                packed.at[first : first + GHOST_LEN, :],
                table_sem.at[1 + j],
            )
        )
    bounds = (0, LAYERS * FAR * ROW_LEN, (LAYERS * FAR + NEAR) * ROW_LEN, SENT * ROW_LEN)
    moved_copies = [
        pltpu.make_async_copy(ref, moved.at[bounds[n] : bounds[n + 1], :], moved_sem.at[n])
        for n, ref in enumerate((far, up, down))
    ]
    left_copies = [
        pltpu.make_async_copy(
            left_hbm.at[:, pl.ds(n * part, part)],
            left.at[:, pl.ds(n * part, part)],
            left_sem.at[n],
        )
        for n in range(PARTS)
    ]
    for copy in table_copies + moved_copies + left_copies:
        copy.start()

    def clear(u, carry):
        for total in totals:
            total[u] = jnp.zeros((B, LANES), f32)
        return carry

    lax.fori_loop(0, U_DEV + 1, clear, 0, unroll=5)

    def expand(c, carry):
        h = packed[pl.ds(pl.multiple_of(c * HALF, HALF), HALF), :]
        turned = swap_lanes(h)
        double[c, 0:HALF, :] = jnp.concatenate([h[:, :B], turned[:, B:]], axis=1)
        double[c, HALF:, :] = jnp.concatenate([turned[:, :B], h[:, B:]], axis=1)
        return carry

    table_copies[0].wait()
    lax.fori_loop(0, ROWS, expand, 0, unroll=8)
    for copy in table_copies[1:]:
        copy.wait()
    lax.fori_loop(ROWS, TABLE, expand, 0, unroll=8)
    for copy in moved_copies:
        copy.wait()

    def arrive(s, carry):
        block = double[moved_rows[0, s], :, :][:, :B]
        base = pl.multiple_of(s * ROW_LEN, HALF)
        h = moved[pl.ds(base + 3 * B, HALF), :]
        chunks = [moved[pl.ds(base + c * B, B), :] for c in range(3)]
        chunks.append(jnp.concatenate([h[:, :B], h[:, B:]], axis=0))
        got = lax.dot_general(
            block, jnp.concatenate(chunks, axis=1), (((0,), (0,)), ((), ())),
            preferred_element_type=f32,
        ).astype(bf16)
        for c in range(3):
            left[c, ROWS + s] = got[:, c * LANES : (c + 1) * LANES]
        left[3, ROWS + s] = jnp.concatenate(
            [got[:, 3 * LANES :], jnp.zeros((B, B), bf16)], axis=1
        )
        return carry

    lax.fori_loop(0, SENT, arrive, 0, unroll=4)

    zero = jnp.zeros((B, LANES), bf16)

    def row(i, n):
        codes = [place[k, n] for k in range(NBR)]
        for quad in range(2):
            some = codes[4 * quad : 4 * quad + 4]
            slots = [code & 255 for code in some]
            tiles = [double[code >> 8] for code in some]
            tiles += [zero] * (4 - len(tiles))
            upper = jnp.concatenate([tiles[0][:, :B], tiles[2][:, B:]], axis=1)
            lower = jnp.concatenate([tiles[1][:, :B], tiles[3][:, B:]], axis=1)
            weights = jnp.concatenate(
                [
                    jnp.concatenate([upper, zero], axis=1),
                    jnp.concatenate([zero, lower], axis=1),
                ],
                axis=0,
            )
            rows = jnp.concatenate([left[2 * quad, i], left[2 * quad + 1, i]], axis=0)
            got = jnp.dot(rows, weights, preferred_element_type=f32)
            for side in range(2):
                for part in range(2):
                    k = side + 2 * part
                    if k < len(some):
                        first = side * LANES + part * B
                        lanes = slice(part * B, (part + 1) * B)
                        value = got[part * B : (part + 1) * B, first : first + B]
                        totals[side][slots[k], :, lanes] += value

    def some_rows(n, carry):
        for r in range(UNROLL):
            i = n * UNROLL + r
            row(i, i)
        return carry

    for n in range(PARTS):
        left_copies[n].wait()
        lax.fori_loop(n * part // UNROLL, (n + 1) * part // UNROLL, some_rows, 0)

    def more_rows(n, carry):
        for r in range(UNROLL):
            s = n * UNROLL + r
            row(ROWS + s, ROWS + s)
        return carry

    lax.fori_loop(0, SENT // UNROLL, more_rows, 0)
    low = lower_lanes((HALF, LANES))
    for v in range(7):

        def gather(q, carry):
            u = v * UCAP + q
            value = acc0[u] + acc1[u]
            top, bottom = value[:HALF], value[HALF:]
            value = jnp.where(low, top, bottom) + pltpu.roll(jnp.where(low, bottom, top), B, 1)
            if v == 0:
                own[q] = value
            else:
                sends[v - 1][q] = value.astype(bf16)
            return carry

        lax.fori_loop(0, UCAP, gather, 0, unroll=4)


def make_sums(moved_rows, place, left, halves, ghosts, far, up, down):
    hbm = pl.BlockSpec(memory_space=pl.ANY)
    block = pl.BlockSpec((UCAP, HALF, LANES), lambda i, *s: (0, 0, 0))
    return pl.pallas_call(
        sums_kernel,
        grid_spec=pltpu.PrefetchScalarGridSpec(
            num_scalar_prefetch=2,
            grid=(1,),
            in_specs=[hbm] * 11,
            out_specs=[block] * 7,
            scratch_shapes=[
                pltpu.VMEM((4, ROWS + SENT, B, LANES), bf16),
                pltpu.VMEM((TABLE * HALF, LANES), bf16),
                pltpu.VMEM((TABLE, B, LANES), bf16),
            ]
            + [pltpu.VMEM((U_DEV + 1, B, LANES), f32)] * 2
            + [
                pltpu.VMEM((SENT * ROW_LEN, LANES), bf16),
                pltpu.SemaphoreType.DMA((PARTS,)),
                pltpu.SemaphoreType.DMA((7,)),
                pltpu.SemaphoreType.DMA((3,)),
            ],
        ),
        out_shape=[jax.ShapeDtypeStruct((UCAP, HALF, LANES), f32)]
        + [jax.ShapeDtypeStruct((UCAP, HALF, LANES), bf16)] * 6,
        compiler_params=pltpu.CompilerParams(vmem_limit_bytes=VMEM_LIMIT),
        cost_estimate=pl.CostEstimate(
            flops=8_000_000_000, transcendentals=0, bytes_accessed=30_000_000
        ),
        name="sums",
    )(moved_rows, place, left, halves, *ghosts, far, up, down)


def final_kernel(numbers, own, r0, r1, r2, r3, r4, r5, out, total):
    parts = (own, r0, r1, r2, r3, r4, r5)
    total[...] = jnp.zeros_like(total)

    def add(q, carry):
        for v in range(7):
            rows = pl.ds(numbers[v, q] * PITCH, HALF)
            total[rows, :] += parts[v][q].astype(f32)
        return carry

    lax.fori_loop(0, UCAP, add, 0, unroll=2)
    low = lower_lanes((8, LANES))

    for g in range(CE_DEV // 8):
        for s in range(16):
            a = total[pl.ds(g * 8 * PITCH + 2 * s, 8, stride=PITCH), :]
            b = total[pl.ds(g * 8 * PITCH + 2 * s + 1, 8, stride=PITCH), :]
            out[g * 8 : g * 8 + 8, s * LANES : (s + 1) * LANES] = jnp.where(
                low, a, pltpu.roll(b, B, 1)
            )
            out[g * 8 : g * 8 + 8, (s + 16) * LANES : (s + 17) * LANES] = jnp.where(
                low, pltpu.roll(a, B, 1), b
            )


def make_final(numbers, parts):
    block = pl.BlockSpec((UCAP, HALF, LANES), lambda i, *s: (0, 0, 0))
    return pl.pallas_call(
        final_kernel,
        grid_spec=pltpu.PrefetchScalarGridSpec(
            num_scalar_prefetch=1,
            grid=(1,),
            in_specs=[block] * 7,
            out_specs=pl.BlockSpec((CE_DEV, B * B), lambda i, *s: (0, 0)),
            scratch_shapes=[pltpu.VMEM((CE_DEV * PITCH, LANES), f32)],
        ),
        out_shape=jax.ShapeDtypeStruct((CE_DEV, B * B), f32),
        compiler_params=pltpu.CompilerParams(vmem_limit_bytes=VMEM_LIMIT),
        name="final",
    )(numbers, *parts)


def neighbour_shift(value, facing):
    axis = AXES[facing // 2]
    return shifted(value, axis, 1 - 2 * (facing % 2))


def one_shard(blocks, prolong, new_owner, arrival, columns, targets, ghost_lists, touched):
    own_layer = lax.axis_index("gz")
    touched_here = touched[0]

    extra = jnp.pad(touched_here, (0, EXTRA * LANES - U_DEV)).reshape(EXTRA, LANES).astype(bf16)
    halves, *outbound = pack(ghost_lists[0], prolong, extra)
    ghosts = []
    for facing in range(6):
        ghosts.append(neighbour_shift(outbound[facing ^ 1], facing ^ 1))

    left, far, up, down = make_left(
        own_layer[None], jnp.stack([arrival, new_owner]), jnp.transpose(blocks, (1, 2, 0)), halves
    )
    far_in = lax.all_to_all(far, "gz", split_axis=0, concat_axis=0, tiled=True)
    up_in = shifted(up, "gz", 1)
    down_in = shifted(down, "gz", -1)

    old = jnp.arange(ROWS, dtype=jnp.int32)
    labels = jnp.arange(LAYERS, dtype=jnp.int32)
    cols = columns.T
    place = jnp.where(cols >= 0, cols * 256 + targets.T, U_DEV)
    ranks = jnp.arange(FAR, dtype=jnp.int32)
    later = FAR + jnp.arange(NEAR, dtype=jnp.int32)
    codes = ROWS + jnp.concatenate(
        [
            (labels[:, None] * CAP + ranks[None, :]).reshape(-1),
            (own_layer - 1) * CAP + later,
            (own_layer + 1) * CAP + later,
        ]
    )
    match = (codes[:, None] == arrival[None, :]) & (codes[:, None] >= ROWS)
    row_of = jnp.sum(jnp.where(match, old[None, :] + 1, 0), axis=1) - 1
    taken = jnp.sum(jnp.where(match[None], place[:, None, :] + 1, 0), axis=2) - 1
    moved_place = jnp.where(row_of[None, :] >= 0, taken, U_DEV)
    place = jnp.concatenate([place, moved_place], axis=1)
    own, *sends = make_sums(
        jnp.maximum(row_of, 0)[None, :], place, left, halves, ghosts,
        far_in.reshape(LAYERS * FAR * ROW_LEN, LANES), up_in, down_in,
    )
    got = [neighbour_shift(sends[facing], facing) for facing in range(6)]

    numbers = [touched_here[:UCAP]]
    for facing in range(6):
        flat = ghosts[facing ^ 1][GHOST_LEN : GHOST_LEN + 2].reshape(-1)
        first = (facing + 1) * UCAP
        numbers.append(flat[first : first + UCAP].astype(jnp.int32))
    return make_final(jnp.stack(numbers), [own] + got)


def solution(mesh):
    return jax.shard_map(
        one_shard,
        mesh=mesh,
        in_specs=(
            P(AXES, None, None),
            P(AXES, None),
            P(AXES),
            P(AXES),
            P(AXES, None),
            P(AXES, None),
            P(AXES, None, None),
            P(AXES, None),
        ),
        out_specs=P(AXES, None),
        check_vma=False,
    )
```

```python
import jax
import jax.numpy as jnp
from jax import lax
from jax.experimental import pallas as pl
from jax.experimental.pallas import tpu as pltpu
from jax.sharding import PartitionSpec as P


B = 64
NBR = 7
CAP = 6
FAR = 2
NEAR = CAP - FAR
GCAP = 64
UCAP = 32
U_DEV = 224
CE_DEV = 64
ROWS = 256
LAYERS = 8
HALF = 32
LANES = 128
AXES = ("gx", "gy", "gz")
SENT = LAYERS * FAR + 2 * NEAR
SENT_PAD = 32
ROW_LEN = 3 * B + HALF
GHOST_LEN = GCAP * HALF
EXTRA = 16
TABLE = ROWS + 6 * GCAP
VMEM_LIMIT = 62 * 1024 * 1024
PITCH = HALF + 1
bf16 = jnp.bfloat16
f32 = jnp.float32


def lower_lanes(shape):
    return lax.broadcasted_iota(jnp.int32, shape, len(shape) - 1) < B


def swap_lanes(v):
    return jnp.concatenate([v[:, B:], v[:, :B]], axis=1)


def shifted(value, axis, by):
    devices = lax.axis_size(axis)
    pairs = [(i, i + by) for i in range(devices) if 0 <= i + by < devices]
    return lax.ppermute(value, axis, pairs)


NEAR_AT = GHOST_LEN + EXTRA
SEND_LEN = [NEAR_AT] * 4 + [NEAR_AT + NEAR * ROW_LEN] * 2
P_PARTS = 4
X_PARTS = 8
NT = (((1,), (1,)), ((), ()))


def pack_kernel(
    layer, lists, owner, touched, prolong_hbm, blocks, halves_out, o0, o1, o2, o3, o4, o5, far_out,
    prolong, halves, v0, v1, v2, v3, v4, v5, far, work, planes, strip0, strip1, strip2, strip3,
    in_sem, plane_sem, out_sem,
):
    sends, outs = (v0, v1, v2, v3, v4, v5), (o0, o1, o2, o3, o4, o5)
    strips = (strip0, strip1, strip2, strip3)
    count, deep = ROWS // P_PARTS, B // X_PARTS

    def prolong_copy(n):
        rows = pl.ds(n * count, count)
        return pltpu.make_async_copy(prolong_hbm.at[rows], prolong.at[rows], in_sem.at[n])

    def plane_copy(n):
        some = pl.ds(n * deep, deep)
        return pltpu.make_async_copy(blocks.at[some], planes.at[some], plane_sem.at[n])

    for n in range(P_PARTS):
        prolong_copy(n).start()
    for n in range(X_PARTS):
        plane_copy(n).start()

    square = (ROWS, ROWS)
    peer = lax.rem(owner[...], LAYERS)
    member = lax.broadcasted_iota(jnp.int32, (16, ROWS), 0) == peer
    earlier = (
        lax.broadcasted_iota(jnp.int32, square, 0) < lax.broadcasted_iota(jnp.int32, square, 1)
    )
    before = jnp.dot(
        member.astype(f32).astype(bf16),
        earlier.astype(f32).astype(bf16),
        preferred_element_type=f32,
    )
    rank = jnp.sum(jnp.where(member, before, 0.0), axis=0, keepdims=True).astype(jnp.int32)
    near_slot = jnp.where(peer > layer[0], LAYERS * FAR, LAYERS * FAR + NEAR) + rank - FAR
    slot = jnp.where(rank < FAR, peer * FAR + rank, near_slot)
    slot = jnp.where(peer == layer[0], -1, slot)
    sent = lax.broadcasted_iota(jnp.int32, (SENT_PAD, ROWS), 0) == slot
    picks = sent.astype(f32).astype(bf16)

    low = lower_lanes((16, LANES))

    def group(g, carry):
        rows = pl.ds(pl.multiple_of(g * 16, 16), 16)
        for s in range(16):
            near = prolong[rows, s * LANES : (s + 1) * LANES].astype(f32)
            far_half = prolong[rows, (s + 16) * LANES : (s + 17) * LANES].astype(f32)
            even = jnp.where(low, near, pltpu.roll(far_half, B, 1))
            odd = jnp.where(low, pltpu.roll(near, B, 1), far_half)
            work[pl.ds(2 * s, 16, stride=PITCH), :] = even
            work[pl.ds(2 * s + 1, 16, stride=PITCH), :] = odd
        for e in range(16):
            halves[pl.ds(pl.multiple_of((g * 16 + e) * HALF, HALF), HALF), :] = work[
                e * PITCH : e * PITCH + HALF, :
            ].astype(bf16)
        return carry

    for n in range(P_PARTS):
        prolong_copy(n).wait()
        lax.fori_loop(n * count // 16, (n + 1) * count // 16, group, 0)
    out_copies = [pltpu.make_async_copy(halves, halves_out, out_sem.at[6])]
    out_copies[0].start()

    top = touched[:, :LANES]
    rest = jnp.concatenate(
        [touched[:, LANES:], jnp.zeros((1, 2 * LANES - U_DEV), jnp.int32)], axis=1
    )
    at = lax.broadcasted_iota(jnp.int32, (EXTRA, LANES), 0)
    extra = jnp.where(at == 0, top, jnp.where(at == 1, rest, 0)).astype(f32).astype(bf16)

    def pick(q, carry):
        for j in range(6):
            row = lists[j, 0, q]
            sends[j][pl.ds(pl.multiple_of(q * HALF, HALF), HALF), :] = halves[
                pl.ds(pl.multiple_of(row * HALF, HALF), HALF), :
            ]
        return carry

    lax.fori_loop(0, GCAP, pick, 0, unroll=4)
    for j in range(6):
        sends[j][GHOST_LEN:NEAR_AT, :] = extra
        out_copies.append(pltpu.make_async_copy(sends[j], outs[j], out_sem.at[j]))
        if j < 4:
            out_copies[-1].start()

    def some_planes(n, carry):
        plane_copy(n).wait()
        for d in range(deep):
            a = n * deep + d
            got = lax.dot_general(picks, planes[a], NT, preferred_element_type=f32)
            rows = pl.ds(a * PITCH, SENT_PAD)
            for c in range(3):
                strips[c][rows, :] = got[:, c * LANES : (c + 1) * LANES]
            strips[3][rows, :B] = got[:, 3 * LANES :]
        return carry

    lax.fori_loop(0, X_PARTS, some_planes, 0)
    for r in range(SENT):
        if r < LAYERS * FAR:
            out, base = far, r * ROW_LEN
        elif r < LAYERS * FAR + NEAR:
            out, base = v4, NEAR_AT + (r - LAYERS * FAR) * ROW_LEN
        else:
            out, base = v5, NEAR_AT + (r - LAYERS * FAR - NEAR) * ROW_LEN
        got = [strip[pl.ds(r, B, stride=PITCH), :].astype(bf16) for strip in strips]
        for c in range(3):
            out[base + c * B : base + (c + 1) * B, :] = got[c]
        out[base + 3 * B : base + ROW_LEN, :] = jnp.concatenate(
            [got[3][:HALF, :B], got[3][HALF:, :B]], axis=1
        )
    out_copies.append(pltpu.make_async_copy(far, far_out, out_sem.at[7]))
    for copy in out_copies[5:]:
        copy.start()
    for copy in out_copies:
        copy.wait()


def pack(layer, lists, owner, touched, prolong, blocks):
    hbm = pl.BlockSpec(memory_space=pl.ANY)
    shapes = [(ROWS * HALF, LANES)] + [(n, LANES) for n in SEND_LEN]
    shapes += [(LAYERS * FAR * ROW_LEN, LANES)]
    return pl.pallas_call(
        pack_kernel,
        grid_spec=pltpu.PrefetchScalarGridSpec(
            num_scalar_prefetch=2,
            grid=(1,),
            in_specs=[
                pl.BlockSpec((1, ROWS), lambda i, *s: (0, 0)),
                pl.BlockSpec((1, U_DEV), lambda i, *s: (0, 0)),
                hbm,
                hbm,
            ],
            out_specs=[hbm] * 8,
            scratch_shapes=[pltpu.VMEM((ROWS, B * B), bf16)]
            + [pltpu.VMEM(shape, bf16) for shape in shapes]
            + [
                pltpu.VMEM((16 * PITCH, LANES), f32),
                pltpu.VMEM((B, NBR * B, ROWS), bf16),
            ]
            + [pltpu.VMEM((B * PITCH, LANES), f32)] * 4
            + [
                pltpu.SemaphoreType.DMA((P_PARTS,)),
                pltpu.SemaphoreType.DMA((X_PARTS,)),
                pltpu.SemaphoreType.DMA((8,)),
            ],
        ),
        out_shape=[jax.ShapeDtypeStruct(shape, bf16) for shape in shapes],
        compiler_params=pltpu.CompilerParams(vmem_limit_bytes=VMEM_LIMIT),
        cost_estimate=pl.CostEstimate(
            flops=2_000_000_000, transcendentals=0, bytes_accessed=23_000_000
        ),
        name="pack",
    )(layer, lists, owner, touched, prolong, blocks)


STEPS = 4
A_STEP = B // STEPS
R_STEP = ROWS // STEPS
TOTAL = ROWS
SPAN = TOTAL + 1


def left_kernel(arrival, blocks, halves, left, table0, table1, transposed, picks):
    j, step = pl.program_id(0), pl.program_id(1)
    tables = (table0, table1)
    square = (ROWS, ROWS)

    @pl.when((j == 0) & (step == 0))
    def _():
        eye = (
            lax.broadcasted_iota(jnp.int32, (B, B), 0)
            == lax.broadcasted_iota(jnp.int32, (B, B), 1)
        ).astype(bf16)

        low = lower_lanes((B, LANES))

        def turn(n, carry):
            tiles = []
            for q in range(4):
                h = halves[pl.ds(pl.multiple_of((n * 4 + q) * HALF, HALF), HALF), :]
                tiles += [h[:, :B], h[:, B:]]
            got = lax.dot_general(
                eye,
                jnp.concatenate(tiles, axis=0),
                (((1,), (1,)), ((), ())),
                preferred_element_type=f32,
            )
            for q in range(4):
                pair = got[:, (q // 2) * LANES : (q // 2 + 1) * LANES]
                mine = low if q % 2 == 0 else jnp.logical_not(low)
                transposed[n * 4 + q] = jnp.where(mine, pair, 0.0).astype(bf16)
            return carry

        lax.fori_loop(0, ROWS // 4, turn, 0, unroll=8)

        down_rows = lax.broadcasted_iota(jnp.int32, square, 0)
        along = lax.broadcasted_iota(jnp.int32, square, 1)
        taken = (down_rows == arrival[...]).astype(f32).astype(bf16)
        unit = (down_rows == along).astype(f32).astype(bf16)
        picks[...] = lax.dot_general(unit, taken, NT, preferred_element_type=f32).astype(bf16)

    @pl.when(step < STEPS)
    def _():
        def relay(n, carry):
            rows = pl.ds((step * A_STEP + n) * SPAN, TOTAL)
            got = lax.dot_general(
                picks[...], blocks[n], (((1,), (1,)), ((), ())), preferred_element_type=f32
            )
            table0[rows, :] = got[:, :LANES]
            table1[rows, :] = got[:, LANES:]
            return carry

        lax.fori_loop(0, A_STEP, relay, 0, unroll=8)

    @pl.when(step >= STEPS)
    def _():
        keep = lower_lanes((B, LANES)) | (j == 0)

        def multiply(n, carry):
            i = (step - STEPS) * R_STEP + 2 * n
            rows = [
                jnp.concatenate(
                    [t[pl.ds(i + q, B, stride=SPAN), :].astype(bf16) for t in tables], axis=1
                )
                for q in range(2)
            ]
            pairs = jnp.concatenate([transposed[i], transposed[i + 1]], axis=0)
            got = jnp.dot(pairs, jnp.concatenate(rows, axis=0), preferred_element_type=f32)
            for q in range(2):
                part = got[q * B : (q + 1) * B]
                left[0, 2 * n + q] = part[:, :LANES].astype(bf16)
                left[1, 2 * n + q] = jnp.where(keep, part[:, LANES:], 0.0).astype(bf16)
            return carry

        lax.fori_loop(0, R_STEP // 2, multiply, 0, unroll=16)


def make_left(arrival, blocks, halves):
    whole = lambda shape: pl.BlockSpec(shape, lambda j, s: (0,) * len(shape))
    return pl.pallas_call(
        left_kernel,
        grid=(2, 2 * STEPS),
        in_specs=[
            whole((1, ROWS)),
            pl.BlockSpec(
                (A_STEP, 2 * LANES, ROWS), lambda j, s: (jnp.minimum(s, STEPS - 1), j, 0)
            ),
            whole((ROWS * HALF, LANES)),
        ],
        out_specs=pl.BlockSpec(
            (2, R_STEP, B, LANES), lambda j, s: (j, jnp.maximum(s - STEPS, 0), 0, 0)
        ),
        out_shape=jax.ShapeDtypeStruct((4, ROWS, B, LANES), bf16),
        scratch_shapes=[
            pltpu.VMEM((B * SPAN, LANES), f32),
            pltpu.VMEM((B * SPAN, LANES), f32),
            pltpu.VMEM((ROWS, B, LANES), bf16),
            pltpu.VMEM((ROWS, ROWS), bf16),
        ],
        compiler_params=pltpu.CompilerParams(
            vmem_limit_bytes=VMEM_LIMIT, dimension_semantics=("arbitrary", "arbitrary")
        ),
        cost_estimate=pl.CostEstimate(
            flops=12_000_000_000, transcendentals=0, bytes_accessed=60_000_000
        ),
        name="left",
    )(arrival, blocks, halves)


PARTS = 8
UNROLL = 16
TALL = B + 1


def sums_kernel(
    moved_rows, columns, targets, left_hbm, halves, g0, g1, g2, g3, g4, g5, far,
    own, fine, s0, s1, s2, s3, s4, s5,
    left, packed, double, acc0, acc1, moved, left_sem, table_sem, moved_sem,
):
    ghosts = (g0, g1, g2, g3, g4, g5)
    sends = (s0, s1, s2, s3, s4, s5)
    totals = (acc0, acc1)
    part = ROWS // PARTS
    table_copies = [pltpu.make_async_copy(halves, packed.at[: ROWS * HALF, :], table_sem.at[0])]
    for j in range(6):
        first = (ROWS + j * GCAP) * HALF
        table_copies.append(
            pltpu.make_async_copy(
                ghosts[j].at[:GHOST_LEN, :],
                packed.at[first : first + GHOST_LEN, :],
                table_sem.at[1 + j],
            )
        )
    first, second = LAYERS * FAR * ROW_LEN, (LAYERS * FAR + NEAR) * ROW_LEN
    moved_copies = [
        pltpu.make_async_copy(far, moved.at[:first, :], moved_sem.at[0]),
        pltpu.make_async_copy(g5.at[NEAR_AT:, :], moved.at[first:second, :], moved_sem.at[1]),
        pltpu.make_async_copy(g4.at[NEAR_AT:, :], moved.at[second:, :], moved_sem.at[2]),
    ]

    def left_copy(n):
        rows = pl.ds(n * part, part)
        return pltpu.make_async_copy(left_hbm.at[:, rows], left.at[:, rows], left_sem.at[n])

    for copy in table_copies + moved_copies:
        copy.start()
    for n in range(PARTS):
        left_copy(n).start()

    def clear(u, carry):
        for total in totals:
            total[pl.ds(u * TALL, TALL), :] = jnp.zeros((TALL, LANES), f32)
        return carry

    lax.fori_loop(0, U_DEV + 1, clear, 0, unroll=5)

    def expand(c, carry):
        h = packed[pl.ds(pl.multiple_of(c * HALF, HALF), HALF), :]
        turned = swap_lanes(h)
        double[c, 0:HALF, :] = jnp.concatenate([h[:, :B], turned[:, B:]], axis=1)
        double[c, HALF:, :] = jnp.concatenate([turned[:, :B], h[:, B:]], axis=1)
        return carry

    table_copies[0].wait()
    lax.fori_loop(0, ROWS, expand, 0, unroll=8)
    for copy in table_copies[1:]:
        copy.wait()
    lax.fori_loop(ROWS, TABLE, expand, 0, unroll=8)
    for copy in moved_copies:
        copy.wait()

    def arrive(s, carry):
        block = double[jnp.maximum(moved_rows[0, s], 0), :, :][:, :B]
        base = pl.multiple_of(s * ROW_LEN, HALF)
        h = moved[pl.ds(base + 3 * B, HALF), :]
        chunks = [moved[pl.ds(base + c * B, B), :] for c in range(3)]
        chunks.append(jnp.concatenate([h[:, :B], h[:, B:]], axis=0))
        got = lax.dot_general(
            block, jnp.concatenate(chunks, axis=1), (((0,), (0,)), ((), ())),
            preferred_element_type=f32,
        ).astype(bf16)
        for c in range(3):
            left[c, ROWS + s] = got[:, c * LANES : (c + 1) * LANES]
        left[3, ROWS + s] = jnp.concatenate(
            [got[:, 3 * LANES :], jnp.zeros((B, B), bf16)], axis=1
        )
        return carry

    lax.fori_loop(0, SENT, arrive, 0, unroll=4)

    zero = jnp.zeros((B, LANES), bf16)

    def row(i, n, valid):
        cols = [columns[k, n] for k in range(NBR)]
        slots_of = [
            jnp.where((cols[k] >= 0) & valid, targets[k, n], U_DEV) for k in range(NBR)
        ]
        for quad in range(2):
            some = cols[4 * quad : 4 * quad + 4]
            slots = slots_of[4 * quad : 4 * quad + 4]
            tiles = [double[jnp.maximum(col, 0)] for col in some]
            tiles += [zero] * (4 - len(tiles))
            upper = jnp.concatenate([tiles[0][:, :B], tiles[2][:, B:]], axis=1)
            lower = jnp.concatenate([tiles[1][:, :B], tiles[3][:, B:]], axis=1)
            weights = jnp.concatenate(
                [
                    jnp.concatenate([upper, zero], axis=1),
                    jnp.concatenate([zero, lower], axis=1),
                ],
                axis=0,
            )
            rows = jnp.concatenate([left[2 * quad, i], left[2 * quad + 1, i]], axis=0)
            got = jnp.dot(rows, weights, preferred_element_type=f32)
            for side in range(2):
                for part in range(2):
                    k = side + 2 * part
                    if k < len(some):
                        first = side * LANES + part * B
                        lanes = slice(part * B, (part + 1) * B)
                        value = got[part * B : (part + 1) * B, first : first + B]
                        totals[side][pl.ds(slots[k] * TALL, B), lanes] += value

    def some_rows(n, carry):
        for r in range(UNROLL):
            row(n * UNROLL + r, n * UNROLL + r, True)
        return carry

    def one_part(n, carry):
        left_copy(n).wait()
        lax.fori_loop(n * (part // UNROLL), (n + 1) * (part // UNROLL), some_rows, 0)
        return carry

    lax.fori_loop(0, PARTS, one_part, 0)

    def more_rows(n, carry):
        for r in range(8):
            source = moved_rows[0, n * 8 + r]
            row(ROWS + n * 8 + r, jnp.maximum(source, 0), source >= 0)
        return carry

    lax.fori_loop(0, SENT // 8, more_rows, 0)
    low = lower_lanes((16, LANES))

    def summed(u, b):
        rows = [pl.ds((u + 8 * n) * TALL + b, 8, stride=TALL) for n in range(2)]
        return jnp.concatenate([acc0[r, :] + acc1[r, :] for r in rows], axis=0)

    for v in range(7):
        for half in range(2):
            u, at = v * UCAP + half * 16, slice(half * 16, half * 16 + 16)

            def gather(s, carry):
                a, b = summed(u, 2 * s), summed(u, 2 * s + 1)
                value = jnp.where(low, a, b) + pltpu.roll(jnp.where(low, b, a), B, 1)
                lanes = pl.ds(pl.multiple_of(s * LANES, LANES), LANES)
                coarse = value.astype(bf16)
                if v == 0:
                    own[at, lanes] = coarse
                    fine[at, lanes] = (value - coarse.astype(f32)).astype(bf16)
                else:
                    sends[v - 1][at, lanes] = coarse
                return carry

            lax.fori_loop(0, HALF, gather, 0, unroll=8)


def make_sums(moved_rows, columns, targets, left, halves, ghosts, far):
    hbm = pl.BlockSpec(memory_space=pl.ANY)
    return pl.pallas_call(
        sums_kernel,
        grid_spec=pltpu.PrefetchScalarGridSpec(
            num_scalar_prefetch=3,
            grid=(1,),
            in_specs=[hbm] * 9,
            out_specs=[pl.BlockSpec((UCAP, B * B), lambda i, *s: (0, 0))] * 8,
            scratch_shapes=[
                pltpu.VMEM((4, ROWS + SENT, B, LANES), bf16),
                pltpu.VMEM((TABLE * HALF, LANES), bf16),
                pltpu.VMEM((TABLE, B, LANES), bf16),
            ]
            + [pltpu.VMEM(((U_DEV + 1) * TALL, LANES), f32)] * 2
            + [
                pltpu.VMEM((SENT * ROW_LEN, LANES), bf16),
                pltpu.SemaphoreType.DMA((PARTS,)),
                pltpu.SemaphoreType.DMA((7,)),
                pltpu.SemaphoreType.DMA((3,)),
            ],
        ),
        out_shape=[jax.ShapeDtypeStruct((UCAP, B * B), bf16)] * 8,
        compiler_params=pltpu.CompilerParams(vmem_limit_bytes=VMEM_LIMIT),
        cost_estimate=pl.CostEstimate(
            flops=8_000_000_000, transcendentals=0, bytes_accessed=30_000_000
        ),
        name="sums",
    )(moved_rows, columns, targets, left, halves, *ghosts, far)


def final_kernel(
    touched, own, fine, r0, r1, r2, r3, r4, r5, g0, g1, g2, g3, g4, g5, out,
    stack, numbers, sem, number_sem,
):
    parts = (own, r0, r1, r2, r3, r4, r5, fine)
    ghosts = (g0, g1, g2, g3, g4, g5)
    copies = [
        pltpu.make_async_copy(
            ghosts[f ^ 1].at[GHOST_LEN:NEAR_AT, :], numbers.at[f], number_sem.at[f]
        )
        for f in range(6)
    ]
    copies += [
        pltpu.make_async_copy(parts[v], stack.at[v * UCAP : (v + 1) * UCAP, :], sem.at[v])
        for v in range(8)
    ]
    for copy in copies:
        copy.start()
    lane = lax.broadcasted_iota(jnp.int32, (1, LANES), 1) // UCAP
    wide = touched[...]
    for copy in copies:
        copy.wait()
    given = [numbers[f].astype(f32) for f in range(6)]
    first = wide[:, :LANES].astype(f32)
    for f in range(3):
        first = jnp.where(lane == f + 1, given[f][0:1, :], first)
    second = jnp.concatenate([wide[:, :UCAP]] * 4, axis=1).astype(f32)
    for f in range(3, 6):
        second = jnp.where(lane == f - 3, given[f][1:2, :], second)
    row = lax.broadcasted_iota(jnp.int32, (CE_DEV, LANES), 0).astype(f32)
    select = jnp.concatenate(
        [(row == first).astype(f32), (row == second).astype(f32)], axis=1
    ).astype(bf16)
    for n in range(8):
        lanes = slice(n * 4 * LANES, (n + 1) * 4 * LANES)
        out[:, lanes] = jnp.dot(select, stack[:, lanes], preferred_element_type=f32)


def make_final(touched, own, fine, got, ghosts):
    hbm = pl.BlockSpec(memory_space=pl.ANY)
    return pl.pallas_call(
        final_kernel,
        grid=(1,),
        in_specs=[pl.BlockSpec((1, U_DEV), lambda i: (0, 0))] + [hbm] * 14,
        out_specs=pl.BlockSpec((CE_DEV, B * B), lambda i: (0, 0)),
        scratch_shapes=[
            pltpu.VMEM((8 * UCAP, B * B), bf16),
            pltpu.VMEM((6, EXTRA, LANES), bf16),
            pltpu.SemaphoreType.DMA((8,)),
            pltpu.SemaphoreType.DMA((6,)),
        ],
        out_shape=jax.ShapeDtypeStruct((CE_DEV, B * B), f32),
        compiler_params=pltpu.CompilerParams(vmem_limit_bytes=VMEM_LIMIT),
        name="final",
    )(touched, own, fine, *got, *ghosts)


def neighbour_shift(value, facing):
    axis = AXES[facing // 2]
    return shifted(value, axis, 1 - 2 * (facing % 2))


def one_shard(blocks, prolong, new_owner, arrival, columns, targets, ghost_lists, touched):
    own_layer = lax.axis_index("gz")
    planes = jnp.transpose(blocks, (1, 2, 0))
    halves, *outbound, far = pack(
        own_layer[None], jnp.transpose(ghost_lists, (1, 0, 2)), new_owner[None], touched,
        prolong, planes,
    )
    ghosts = []
    for facing in range(6):
        ghosts.append(neighbour_shift(outbound[facing ^ 1], facing ^ 1))
    far_in = lax.all_to_all(
        far.reshape(LAYERS, FAR * ROW_LEN, LANES), "gz", split_axis=0, concat_axis=0, tiled=True
    )
    left = make_left(arrival[None], planes, halves)

    old = jnp.arange(ROWS, dtype=jnp.int32)
    labels = jnp.arange(LAYERS, dtype=jnp.int32)
    ranks = jnp.arange(FAR, dtype=jnp.int32)
    later = FAR + jnp.arange(NEAR, dtype=jnp.int32)
    codes = ROWS + jnp.concatenate(
        [
            (labels[:, None] * CAP + ranks[None, :]).reshape(-1),
            (own_layer - 1) * CAP + later,
            (own_layer + 1) * CAP + later,
        ]
    )
    match = (codes[:, None] == arrival[None, :]) & (codes[:, None] >= ROWS)
    row_of = jnp.sum(jnp.where(match, old[None, :] + 1, 0), axis=1) - 1
    own, fine, *sends = make_sums(
        row_of[None, :], columns.T, targets.T, left, halves, ghosts,
        far_in.reshape(LAYERS * FAR * ROW_LEN, LANES),
    )
    got = [neighbour_shift(sends[facing], facing) for facing in range(6)]
    return make_final(touched, own, fine, got, ghosts)


def solution(mesh):
    return jax.shard_map(
        one_shard,
        mesh=mesh,
        in_specs=(
            P(AXES, None, None),
            P(AXES, None),
            P(AXES),
            P(AXES),
            P(AXES, None),
            P(AXES, None),
            P(AXES, None, None),
            P(AXES, None),
        ),
        out_specs=P(AXES, None),
        check_vma=False,
    )
```

```python
import jax
import jax.numpy as jnp
from jax import lax
from jax.experimental import pallas as pl
from jax.experimental.pallas import tpu as pltpu
from jax.sharding import PartitionSpec as P


B = 64
NBR = 7
CAP = 6
FAR = 2
NEAR = CAP - FAR
GCAP = 64
UCAP = 32
U_DEV = 224
CE_DEV = 64
ROWS = 256
LAYERS = 8
HALF = 32
LANES = 128
AXES = ("gx", "gy", "gz")
SENT = LAYERS * FAR + 2 * NEAR
SENT_PAD = 32
ROW_LEN = 3 * B + HALF
GHOST_LEN = GCAP * HALF
EXTRA = 16
TABLE = ROWS + 6 * GCAP
VMEM_LIMIT = 62 * 1024 * 1024
PITCH = HALF + 1
bf16 = jnp.bfloat16
f32 = jnp.float32


def lower_lanes(shape):
    return lax.broadcasted_iota(jnp.int32, shape, len(shape) - 1) < B


def shifted(value, axis, by):
    devices = lax.axis_size(axis)
    pairs = [(i, i + by) for i in range(devices) if 0 <= i + by < devices]
    return lax.ppermute(value, axis, pairs)


NEAR_AT = GHOST_LEN + EXTRA
SEND_LEN = [NEAR_AT] * 4 + [NEAR_AT + NEAR * ROW_LEN] * 2
P_PARTS = 4
X_PARTS = 8
NT = (((1,), (1,)), ((), ()))


def pack_kernel(
    layer, lists, owner, touched, prolong_hbm, blocks, halves_out, o0, o1, o2, o3, o4, o5, far_out,
    prolong, halves, v0, v1, v2, v3, v4, v5, far, work, planes, strip0, strip1, strip2, strip3,
    in_sem, plane_sem, out_sem,
):
    sends, outs = (v0, v1, v2, v3, v4, v5), (o0, o1, o2, o3, o4, o5)
    strips = (strip0, strip1, strip2, strip3)
    count, deep = ROWS // P_PARTS, B // X_PARTS

    def prolong_copy(n):
        rows = pl.ds(n * count, count)
        return pltpu.make_async_copy(prolong_hbm.at[rows], prolong.at[rows], in_sem.at[n])

    def plane_copy(n):
        some = pl.ds(n * deep, deep)
        return pltpu.make_async_copy(blocks.at[some], planes.at[some], plane_sem.at[n])

    for n in range(P_PARTS):
        prolong_copy(n).start()
    square = (ROWS, ROWS)
    peer = lax.rem(owner[...], LAYERS)
    member = lax.broadcasted_iota(jnp.int32, (16, ROWS), 0) == peer
    earlier = (
        lax.broadcasted_iota(jnp.int32, square, 0) < lax.broadcasted_iota(jnp.int32, square, 1)
    )
    before = jnp.dot(
        member.astype(f32).astype(bf16),
        earlier.astype(f32).astype(bf16),
        preferred_element_type=f32,
    )
    rank = jnp.sum(jnp.where(member, before, 0.0), axis=0, keepdims=True).astype(jnp.int32)
    near_slot = jnp.where(peer > layer[0], LAYERS * FAR, LAYERS * FAR + NEAR) + rank - FAR
    slot = jnp.where(rank < FAR, peer * FAR + rank, near_slot)
    slot = jnp.where(peer == layer[0], -1, slot)
    sent = lax.broadcasted_iota(jnp.int32, (SENT_PAD, ROWS), 0) == slot
    picks = sent.astype(f32).astype(bf16)

    low = lower_lanes((16, LANES))

    def group(g, carry):
        rows = pl.ds(pl.multiple_of(g * 16, 16), 16)
        for s in range(16):
            near = prolong[rows, s * LANES : (s + 1) * LANES].astype(f32)
            far_half = prolong[rows, (s + 16) * LANES : (s + 17) * LANES].astype(f32)
            even = jnp.where(low, near, pltpu.roll(far_half, B, 1))
            odd = jnp.where(low, pltpu.roll(near, B, 1), far_half)
            work[pl.ds(2 * s, 16, stride=PITCH), :] = even
            work[pl.ds(2 * s + 1, 16, stride=PITCH), :] = odd
        for e in range(16):
            halves[pl.ds(pl.multiple_of((g * 16 + e) * HALF, HALF), HALF), :] = work[
                e * PITCH : e * PITCH + HALF, :
            ].astype(bf16)
        return carry

    for n in range(P_PARTS):
        prolong_copy(n).wait()
        if n == 0:
            for m in range(X_PARTS):
                plane_copy(m).start()
        lax.fori_loop(n * count // 16, (n + 1) * count // 16, group, 0)
    out_copies = [pltpu.make_async_copy(halves, halves_out, out_sem.at[6])]
    out_copies[0].start()

    top = touched[:, :LANES]
    rest = jnp.concatenate(
        [touched[:, LANES:], jnp.zeros((1, 2 * LANES - U_DEV), jnp.int32)], axis=1
    )
    at = lax.broadcasted_iota(jnp.int32, (EXTRA, LANES), 0)
    extra = jnp.where(at == 0, top, jnp.where(at == 1, rest, 0)).astype(f32).astype(bf16)

    def pick(q):
        for j in range(6):
            row = lists[j, 0, q]
            sends[j][pl.ds(pl.multiple_of(q * HALF, HALF), HALF), :] = halves[
                pl.ds(pl.multiple_of(row * HALF, HALF), HALF), :
            ]

    def some_planes(n, carry):
        plane_copy(n).wait()
        for d in range(deep):
            a = n * deep + d
            got = lax.dot_general(picks, planes[a], NT, preferred_element_type=f32)
            rows = pl.ds(a * PITCH, SENT_PAD)
            for c in range(3):
                strips[c][rows, :] = got[:, c * LANES : (c + 1) * LANES]
            strips[3][rows, :B] = got[:, 3 * LANES :]
            pick(a)
        return carry

    lax.fori_loop(0, X_PARTS, some_planes, 0)
    for j in range(6):
        sends[j][GHOST_LEN:NEAR_AT, :] = extra
        out_copies.append(pltpu.make_async_copy(sends[j], outs[j], out_sem.at[j]))
        if j < 4:
            out_copies[-1].start()
    for r in range(SENT):
        if r < LAYERS * FAR:
            out, base = far, r * ROW_LEN
        elif r < LAYERS * FAR + NEAR:
            out, base = v4, NEAR_AT + (r - LAYERS * FAR) * ROW_LEN
        else:
            out, base = v5, NEAR_AT + (r - LAYERS * FAR - NEAR) * ROW_LEN
        got = [strip[pl.ds(r, B, stride=PITCH), :].astype(bf16) for strip in strips]
        for c in range(3):
            out[base + c * B : base + (c + 1) * B, :] = got[c]
        out[base + 3 * B : base + ROW_LEN, :] = jnp.concatenate(
            [got[3][:HALF, :B], got[3][HALF:, :B]], axis=1
        )
    out_copies.append(pltpu.make_async_copy(far, far_out, out_sem.at[7]))
    for copy in out_copies[5:]:
        copy.start()
    for copy in out_copies:
        copy.wait()


def pack(layer, lists, owner, touched, prolong, blocks):
    hbm = pl.BlockSpec(memory_space=pl.ANY)
    shapes = [(ROWS * HALF, LANES)] + [(n, LANES) for n in SEND_LEN]
    shapes += [(LAYERS * FAR * ROW_LEN, LANES)]
    return pl.pallas_call(
        pack_kernel,
        grid_spec=pltpu.PrefetchScalarGridSpec(
            num_scalar_prefetch=2,
            grid=(1,),
            in_specs=[
                pl.BlockSpec((1, ROWS), lambda i, *s: (0, 0)),
                pl.BlockSpec((1, U_DEV), lambda i, *s: (0, 0)),
                hbm,
                hbm,
            ],
            out_specs=[hbm] * 8,
            scratch_shapes=[pltpu.VMEM((ROWS, B * B), bf16)]
            + [pltpu.VMEM(shape, bf16) for shape in shapes]
            + [
                pltpu.VMEM((16 * PITCH, LANES), f32),
                pltpu.VMEM((B, NBR * B, ROWS), bf16),
            ]
            + [pltpu.VMEM((B * PITCH, LANES), f32)] * 4
            + [
                pltpu.SemaphoreType.DMA((P_PARTS,)),
                pltpu.SemaphoreType.DMA((X_PARTS,)),
                pltpu.SemaphoreType.DMA((8,)),
            ],
        ),
        out_shape=[jax.ShapeDtypeStruct(shape, bf16) for shape in shapes],
        compiler_params=pltpu.CompilerParams(vmem_limit_bytes=VMEM_LIMIT),
        cost_estimate=pl.CostEstimate(
            flops=2_000_000_000, transcendentals=0, bytes_accessed=23_000_000
        ),
        name="pack",
    )(layer, lists, owner, touched, prolong, blocks)


STEPS = 4
A_STEP = B // STEPS
R_STEP = ROWS // STEPS
TOTAL = ROWS
SPAN = TOTAL + 1


def left_kernel(arrival, blocks, halves, left, table0, table1, transposed, picks):
    j, step = pl.program_id(0), pl.program_id(1)
    tables = (table0, table1)
    square = (ROWS, ROWS)

    @pl.when((j == 0) & (step == 0))
    def _():
        eye = (
            lax.broadcasted_iota(jnp.int32, (B, B), 0)
            == lax.broadcasted_iota(jnp.int32, (B, B), 1)
        ).astype(bf16)

        low = lower_lanes((B, LANES))

        def turn(n, carry):
            tiles = []
            for q in range(4):
                h = halves[pl.ds(pl.multiple_of((n * 4 + q) * HALF, HALF), HALF), :]
                tiles += [h[:, :B], h[:, B:]]
            got = lax.dot_general(
                eye,
                jnp.concatenate(tiles, axis=0),
                (((1,), (1,)), ((), ())),
                preferred_element_type=f32,
            )
            for q in range(4):
                pair = got[:, (q // 2) * LANES : (q // 2 + 1) * LANES]
                mine = low if q % 2 == 0 else jnp.logical_not(low)
                transposed[n * 4 + q] = jnp.where(mine, pair, 0.0).astype(bf16)
            return carry

        lax.fori_loop(0, ROWS // 4, turn, 0, unroll=8)

        down_rows = lax.broadcasted_iota(jnp.int32, square, 0)
        along = lax.broadcasted_iota(jnp.int32, square, 1)
        taken = (down_rows == arrival[...]).astype(f32).astype(bf16)
        unit = (down_rows == along).astype(f32).astype(bf16)
        picks[...] = lax.dot_general(unit, taken, NT, preferred_element_type=f32).astype(bf16)

    def relay(width):
        def plane(n, carry):
            rows = pl.ds((step * A_STEP + n) * SPAN, TOTAL)
            got = lax.dot_general(
                picks[...], blocks[n, :width], NT, preferred_element_type=f32
            )
            table0[rows, :] = got[:, :LANES]
            table1[rows, : width - LANES] = got[:, LANES:]
            return carry

        lax.fori_loop(0, A_STEP, plane, 0, unroll=16)

    @pl.when((step < STEPS) & (j == 0))
    def _():
        relay(2 * LANES)

    @pl.when((step < STEPS) & (j == 1))
    def _():
        relay(LANES + B)

    @pl.when(step >= STEPS)
    def _():
        def multiply(n, carry):
            i = (step - STEPS) * R_STEP + 2 * n
            rows = [
                jnp.concatenate(
                    [t[pl.ds(i + q, B, stride=SPAN), :].astype(bf16) for t in tables], axis=1
                )
                for q in range(2)
            ]
            pairs = jnp.concatenate([transposed[i], transposed[i + 1]], axis=0)
            got = jnp.dot(pairs, jnp.concatenate(rows, axis=0), preferred_element_type=f32)
            for q in range(2):
                part = got[q * B : (q + 1) * B]
                left[0, 2 * n + q] = part[:, :LANES].astype(bf16)
                left[1, 2 * n + q] = part[:, LANES:].astype(bf16)
            return carry

        lax.fori_loop(0, R_STEP // 2, multiply, 0, unroll=32)


def make_left(arrival, blocks, halves):
    whole = lambda shape: pl.BlockSpec(shape, lambda j, s: (0,) * len(shape))
    return pl.pallas_call(
        left_kernel,
        grid=(2, 2 * STEPS),
        in_specs=[
            whole((1, ROWS)),
            pl.BlockSpec(
                (A_STEP, 2 * LANES, ROWS), lambda j, s: (jnp.minimum(s, STEPS - 1), j, 0)
            ),
            whole((ROWS * HALF, LANES)),
        ],
        out_specs=pl.BlockSpec(
            (2, R_STEP, B, LANES), lambda j, s: (j, jnp.maximum(s - STEPS, 0), 0, 0)
        ),
        out_shape=jax.ShapeDtypeStruct((4, ROWS, B, LANES), bf16),
        scratch_shapes=[
            pltpu.VMEM((B * SPAN, LANES), f32),
            pltpu.VMEM((B * SPAN, LANES), f32),
            pltpu.VMEM((ROWS, B, LANES), bf16),
            pltpu.VMEM((ROWS, ROWS), bf16),
        ],
        compiler_params=pltpu.CompilerParams(
            vmem_limit_bytes=VMEM_LIMIT, dimension_semantics=("arbitrary", "arbitrary")
        ),
        cost_estimate=pl.CostEstimate(
            flops=12_000_000_000, transcendentals=0, bytes_accessed=60_000_000
        ),
        name="left",
    )(arrival, blocks, halves)


PARTS = 8
UNROLL = 32
TALL = B + 1


def sums_kernel(
    moved_rows, columns, targets, left_hbm, halves, g0, g1, g2, g3, g4, g5, far,
    own, fine, s0, s1, s2, s3, s4, s5,
    left, packed, acc0, acc1, moved, left_sem, table_sem, moved_sem,
):
    ghosts = (g0, g1, g2, g3, g4, g5)
    sends = (s0, s1, s2, s3, s4, s5)
    totals = (acc0, acc1)
    part = ROWS // PARTS
    table_copies = [pltpu.make_async_copy(halves, packed.at[: ROWS * HALF, :], table_sem.at[0])]
    for j in range(6):
        first = (ROWS + j * GCAP) * HALF
        table_copies.append(
            pltpu.make_async_copy(
                ghosts[j].at[:GHOST_LEN, :],
                packed.at[first : first + GHOST_LEN, :],
                table_sem.at[1 + j],
            )
        )
    first, second = LAYERS * FAR * ROW_LEN, (LAYERS * FAR + NEAR) * ROW_LEN
    moved_copies = [
        pltpu.make_async_copy(far, moved.at[:first, :], moved_sem.at[0]),
        pltpu.make_async_copy(g5.at[NEAR_AT:, :], moved.at[first:second, :], moved_sem.at[1]),
        pltpu.make_async_copy(g4.at[NEAR_AT:, :], moved.at[second:, :], moved_sem.at[2]),
    ]

    def left_copy(n):
        rows = pl.ds(n * part, part)
        return pltpu.make_async_copy(left_hbm.at[:, rows], left.at[:, rows], left_sem.at[n])

    for copy in table_copies + moved_copies:
        copy.start()
    for n in range(PARTS):
        left_copy(n).start()

    def clear(u, carry):
        for total in totals:
            total[pl.ds(u * TALL, TALL), :] = jnp.zeros((TALL, LANES), f32)
        return carry

    lax.fori_loop(0, U_DEV + 1, clear, 0, unroll=5)

    def tile(c):
        return packed[pl.ds(pl.multiple_of(c * HALF, HALF), HALF), :]

    def beside(p, q):
        return jnp.concatenate(
            [
                jnp.concatenate([p[:, :B], q[:, :B]], axis=1),
                jnp.concatenate([p[:, B:], q[:, B:]], axis=1),
            ],
            axis=0,
        )

    for copy in table_copies + moved_copies:
        copy.wait()

    def arrive(s, carry):
        own_tile = tile(jnp.maximum(moved_rows[0, s], 0))
        block = jnp.concatenate([own_tile[:, :B], own_tile[:, B:]], axis=0)
        base = pl.multiple_of(s * ROW_LEN, HALF)
        h = moved[pl.ds(base + 3 * B, HALF), :]
        chunks = [moved[pl.ds(base + c * B, B), :] for c in range(3)]
        chunks.append(jnp.concatenate([h[:, :B], h[:, B:]], axis=0))
        got = lax.dot_general(
            block, jnp.concatenate(chunks, axis=1), (((0,), (0,)), ((), ())),
            preferred_element_type=f32,
        ).astype(bf16)
        for c in range(3):
            left[c, ROWS + s] = got[:, c * LANES : (c + 1) * LANES]
        left[3, ROWS + s] = jnp.concatenate(
            [got[:, 3 * LANES :], jnp.zeros((B, B), bf16)], axis=1
        )
        return carry

    lax.fori_loop(0, SENT, arrive, 0, unroll=8)

    zero = jnp.zeros((B, LANES), bf16)

    def row(i, n, valid):
        cols = [columns[k, n] for k in range(NBR)]
        slots_of = [
            jnp.where((cols[k] >= 0) & valid, targets[k, n], U_DEV) for k in range(NBR)
        ]
        for quad in range(2):
            some = cols[4 * quad : 4 * quad + 4]
            slots = slots_of[4 * quad : 4 * quad + 4]
            tiles = [tile(jnp.maximum(col, 0)) for col in some]
            tiles += [zero[:HALF]] * (4 - len(tiles))
            upper, lower = beside(tiles[0], tiles[2]), beside(tiles[1], tiles[3])
            weights = jnp.concatenate(
                [
                    jnp.concatenate([upper, zero], axis=1),
                    jnp.concatenate([zero, lower], axis=1),
                ],
                axis=0,
            )
            rows = jnp.concatenate([left[2 * quad, i], left[2 * quad + 1, i]], axis=0)
            got = jnp.dot(rows, weights, preferred_element_type=f32)
            for side in range(2):
                for part in range(2):
                    k = side + 2 * part
                    if k < len(some):
                        first = side * LANES + part * B
                        lanes = slice(part * B, (part + 1) * B)
                        value = got[part * B : (part + 1) * B, first : first + B]
                        totals[side][pl.ds(slots[k] * TALL, B), lanes] += value

    def some_rows(n, carry):
        for r in range(UNROLL):
            row(n * UNROLL + r, n * UNROLL + r, True)
        return carry

    def one_part(n, carry):
        left_copy(n).wait()
        lax.fori_loop(n * (part // UNROLL), (n + 1) * (part // UNROLL), some_rows, 0)
        return carry

    lax.fori_loop(0, PARTS, one_part, 0)

    def more_rows(n, carry):
        for r in range(8):
            source = moved_rows[0, n * 8 + r]
            row(ROWS + n * 8 + r, jnp.maximum(source, 0), source >= 0)
        return carry

    lax.fori_loop(0, SENT // 8, more_rows, 0)
    low = lower_lanes((16, LANES))

    def summed(u, b):
        rows = [pl.ds((u + 8 * n) * TALL + b, 8, stride=TALL) for n in range(2)]
        return jnp.concatenate([acc0[r, :] + acc1[r, :] for r in rows], axis=0)

    for v in range(7):
        for half in range(2):
            u, at = v * UCAP + half * 16, slice(half * 16, half * 16 + 16)

            def gather(s, carry):
                a, b = summed(u, 2 * s), summed(u, 2 * s + 1)
                value = jnp.where(low, a, b) + pltpu.roll(jnp.where(low, b, a), B, 1)
                lanes = pl.ds(pl.multiple_of(s * LANES, LANES), LANES)
                coarse = value.astype(bf16)
                if v == 0:
                    own[at, lanes] = coarse
                    fine[at, lanes] = (value - coarse.astype(f32)).astype(bf16)
                else:
                    sends[v - 1][at, lanes] = coarse
                return carry

            lax.fori_loop(0, HALF, gather, 0, unroll=16)


def make_sums(moved_rows, columns, targets, left, halves, ghosts, far):
    hbm = pl.BlockSpec(memory_space=pl.ANY)
    return pl.pallas_call(
        sums_kernel,
        grid_spec=pltpu.PrefetchScalarGridSpec(
            num_scalar_prefetch=3,
            grid=(1,),
            in_specs=[hbm] * 9,
            out_specs=[pl.BlockSpec((UCAP, B * B), lambda i, *s: (0, 0))] * 8,
            scratch_shapes=[
                pltpu.VMEM((4, ROWS + SENT, B, LANES), bf16),
                pltpu.VMEM((TABLE * HALF, LANES), bf16),
            ]
            + [pltpu.VMEM(((U_DEV + 1) * TALL, LANES), f32)] * 2
            + [
                pltpu.VMEM((SENT * ROW_LEN, LANES), bf16),
                pltpu.SemaphoreType.DMA((PARTS,)),
                pltpu.SemaphoreType.DMA((7,)),
                pltpu.SemaphoreType.DMA((3,)),
            ],
        ),
        out_shape=[jax.ShapeDtypeStruct((UCAP, B * B), bf16)] * 8,
        compiler_params=pltpu.CompilerParams(vmem_limit_bytes=VMEM_LIMIT),
        cost_estimate=pl.CostEstimate(
            flops=8_000_000_000, transcendentals=0, bytes_accessed=30_000_000
        ),
        name="sums",
    )(moved_rows, columns, targets, left, halves, *ghosts, far)


def final_kernel(
    touched, own, fine, r0, r1, r2, r3, r4, r5, g0, g1, g2, g3, g4, g5, out,
    stack, numbers, sem, number_sem,
):
    parts = (own, r0, r1, r2, r3, r4, r5, fine)
    ghosts = (g0, g1, g2, g3, g4, g5)
    copies = [
        pltpu.make_async_copy(
            ghosts[f ^ 1].at[GHOST_LEN:NEAR_AT, :], numbers.at[f], number_sem.at[f]
        )
        for f in range(6)
    ]
    copies += [
        pltpu.make_async_copy(parts[v], stack.at[v * UCAP : (v + 1) * UCAP, :], sem.at[v])
        for v in range(8)
    ]
    for copy in copies:
        copy.start()
    lane = lax.broadcasted_iota(jnp.int32, (1, LANES), 1) // UCAP
    wide = touched[...]
    for copy in copies:
        copy.wait()
    given = [numbers[f].astype(f32) for f in range(6)]
    first = wide[:, :LANES].astype(f32)
    for f in range(3):
        first = jnp.where(lane == f + 1, given[f][0:1, :], first)
    second = jnp.concatenate([wide[:, :UCAP]] * 4, axis=1).astype(f32)
    for f in range(3, 6):
        second = jnp.where(lane == f - 3, given[f][1:2, :], second)
    row = lax.broadcasted_iota(jnp.int32, (CE_DEV, LANES), 0).astype(f32)
    select = jnp.concatenate(
        [(row == first).astype(f32), (row == second).astype(f32)], axis=1
    ).astype(bf16)
    for n in range(8):
        lanes = slice(n * 4 * LANES, (n + 1) * 4 * LANES)
        out[:, lanes] = jnp.dot(select, stack[:, lanes], preferred_element_type=f32)


def make_final(touched, own, fine, got, ghosts):
    hbm = pl.BlockSpec(memory_space=pl.ANY)
    return pl.pallas_call(
        final_kernel,
        grid=(1,),
        in_specs=[pl.BlockSpec((1, U_DEV), lambda i: (0, 0))] + [hbm] * 14,
        out_specs=pl.BlockSpec((CE_DEV, B * B), lambda i: (0, 0)),
        scratch_shapes=[
            pltpu.VMEM((8 * UCAP, B * B), bf16),
            pltpu.VMEM((6, EXTRA, LANES), bf16),
            pltpu.SemaphoreType.DMA((8,)),
            pltpu.SemaphoreType.DMA((6,)),
        ],
        out_shape=jax.ShapeDtypeStruct((CE_DEV, B * B), f32),
        compiler_params=pltpu.CompilerParams(vmem_limit_bytes=VMEM_LIMIT),
        name="final",
    )(touched, own, fine, *got, *ghosts)


def neighbour_shift(value, facing):
    axis = AXES[facing // 2]
    return shifted(value, axis, 1 - 2 * (facing % 2))


def one_shard(blocks, prolong, new_owner, arrival, columns, targets, ghost_lists, touched):
    own_layer = lax.axis_index("gz")
    planes = jnp.transpose(blocks, (1, 2, 0))
    halves, *outbound, far = pack(
        own_layer[None], jnp.transpose(ghost_lists, (1, 0, 2)), new_owner[None], touched,
        prolong, planes,
    )
    ghosts = []
    for facing in range(6):
        ghosts.append(neighbour_shift(outbound[facing ^ 1], facing ^ 1))
    far_in = lax.all_to_all(
        far.reshape(LAYERS, FAR * ROW_LEN, LANES), "gz", split_axis=0, concat_axis=0, tiled=True
    )
    left = make_left(arrival[None], planes, halves)

    old = jnp.arange(ROWS, dtype=jnp.int32)
    labels = jnp.arange(LAYERS, dtype=jnp.int32)
    ranks = jnp.arange(FAR, dtype=jnp.int32)
    later = FAR + jnp.arange(NEAR, dtype=jnp.int32)
    codes = ROWS + jnp.concatenate(
        [
            (labels[:, None] * CAP + ranks[None, :]).reshape(-1),
            (own_layer - 1) * CAP + later,
            (own_layer + 1) * CAP + later,
        ]
    )
    match = (codes[:, None] == arrival[None, :]) & (codes[:, None] >= ROWS)
    row_of = jnp.sum(jnp.where(match, old[None, :] + 1, 0), axis=1) - 1
    own, fine, *sends = make_sums(
        row_of[None, :], columns.T, targets.T, left, halves, ghosts,
        far_in.reshape(LAYERS * FAR * ROW_LEN, LANES),
    )
    got = [neighbour_shift(sends[facing], facing) for facing in range(6)]
    return make_final(touched, own, fine, got, ghosts)


def solution(mesh):
    return jax.shard_map(
        one_shard,
        mesh=mesh,
        in_specs=(
            P(AXES, None, None),
            P(AXES, None),
            P(AXES),
            P(AXES),
            P(AXES, None),
            P(AXES, None),
            P(AXES, None, None),
            P(AXES, None),
        ),
        out_specs=P(AXES, None),
        check_vma=False,
    )
```

```python
import jax
import jax.numpy as jnp
from jax import lax
from jax.experimental import pallas as pl
from jax.experimental.pallas import tpu as pltpu
from jax.sharding import PartitionSpec as P


B = 64
NBR = 7
CAP = 6
FAR = 2
NEAR = CAP - FAR
GCAP = 64
UCAP = 32
U_DEV = 224
CE_DEV = 64
ROWS = 256
LAYERS = 8
HALF = 32
LANES = 128
AXES = ("gx", "gy", "gz")
SENT = LAYERS * FAR + 2 * NEAR
SENT_PAD = 32
ROW_LEN = 3 * B + HALF
GHOST_LEN = GCAP * HALF
EXTRA = 16
TABLE = ROWS + 6 * GCAP
VMEM_LIMIT = 62 * 1024 * 1024
PITCH = HALF + 1
bf16 = jnp.bfloat16
f32 = jnp.float32


def lower_lanes(shape):
    return lax.broadcasted_iota(jnp.int32, shape, len(shape) - 1) < B


def shifted(value, axis, by):
    devices = lax.axis_size(axis)
    pairs = [(i, i + by) for i in range(devices) if 0 <= i + by < devices]
    return lax.ppermute(value, axis, pairs)


NEAR_AT = GHOST_LEN + EXTRA
SEND_LEN = [NEAR_AT] * 4 + [NEAR_AT + NEAR * ROW_LEN] * 2
P_PARTS = 4
X_PARTS = 8
NT = (((1,), (1,)), ((), ()))


def pack_kernel(
    layer, lists, owner, touched, prolong_hbm, blocks, halves_out, o0, o1, o2, o3, o4, o5, far_out,
    prolong, halves, v0, v1, v2, v3, v4, v5, far, work, planes, strip0, strip1, strip2, strip3,
    in_sem, plane_sem, out_sem,
):
    sends, outs = (v0, v1, v2, v3, v4, v5), (o0, o1, o2, o3, o4, o5)
    strips = (strip0, strip1, strip2, strip3)
    count, deep = ROWS // P_PARTS, B // X_PARTS

    def prolong_copy(n):
        rows = pl.ds(n * count, count)
        return pltpu.make_async_copy(prolong_hbm.at[rows], prolong.at[rows], in_sem.at[n])

    def plane_copy(n):
        some = pl.ds(n * deep, deep)
        return pltpu.make_async_copy(blocks.at[some], planes.at[some], plane_sem.at[n])

    for n in range(P_PARTS):
        prolong_copy(n).start()
    square = (ROWS, ROWS)
    peer = lax.rem(owner[...], LAYERS)
    member = lax.broadcasted_iota(jnp.int32, (16, ROWS), 0) == peer
    earlier = (
        lax.broadcasted_iota(jnp.int32, square, 0) < lax.broadcasted_iota(jnp.int32, square, 1)
    )
    before = jnp.dot(
        member.astype(f32).astype(bf16),
        earlier.astype(f32).astype(bf16),
        preferred_element_type=f32,
    )
    rank = jnp.sum(jnp.where(member, before, 0.0), axis=0, keepdims=True).astype(jnp.int32)
    near_slot = jnp.where(peer > layer[0], LAYERS * FAR, LAYERS * FAR + NEAR) + rank - FAR
    slot = jnp.where(rank < FAR, peer * FAR + rank, near_slot)
    slot = jnp.where(peer == layer[0], -1, slot)
    sent = lax.broadcasted_iota(jnp.int32, (SENT_PAD, ROWS), 0) == slot
    picks = sent.astype(f32).astype(bf16)

    low = lower_lanes((16, LANES))

    def group(g, carry):
        rows = pl.ds(pl.multiple_of(g * 16, 16), 16)
        for s in range(16):
            near = prolong[rows, s * LANES : (s + 1) * LANES].astype(f32)
            far_half = prolong[rows, (s + 16) * LANES : (s + 17) * LANES].astype(f32)
            even = jnp.where(low, near, pltpu.roll(far_half, B, 1))
            odd = jnp.where(low, pltpu.roll(near, B, 1), far_half)
            work[pl.ds(2 * s, 16, stride=PITCH), :] = even
            work[pl.ds(2 * s + 1, 16, stride=PITCH), :] = odd
        for e in range(16):
            halves[pl.ds(pl.multiple_of((g * 16 + e) * HALF, HALF), HALF), :] = work[
                e * PITCH : e * PITCH + HALF, :
            ].astype(bf16)
        return carry

    for n in range(P_PARTS):
        prolong_copy(n).wait()
        if n == 0:
            for m in range(X_PARTS):
                plane_copy(m).start()
        lax.fori_loop(n * count // 16, (n + 1) * count // 16, group, 0)
    out_copies = [pltpu.make_async_copy(halves, halves_out, out_sem.at[6])]
    out_copies[0].start()

    top = touched[:, :LANES]
    rest = jnp.concatenate(
        [touched[:, LANES:], jnp.zeros((1, 2 * LANES - U_DEV), jnp.int32)], axis=1
    )
    at = lax.broadcasted_iota(jnp.int32, (EXTRA, LANES), 0)
    extra = jnp.where(at == 0, top, jnp.where(at == 1, rest, 0)).astype(f32).astype(bf16)

    def pick(q):
        for j in range(6):
            row = lists[j, 0, q]
            sends[j][pl.ds(pl.multiple_of(q * HALF, HALF), HALF), :] = halves[
                pl.ds(pl.multiple_of(row * HALF, HALF), HALF), :
            ]

    def some_planes(n, carry):
        plane_copy(n).wait()
        for d in range(deep):
            a = n * deep + d
            got = lax.dot_general(picks, planes[a], NT, preferred_element_type=f32)
            rows = pl.ds(a * PITCH, SENT_PAD)
            for c in range(3):
                strips[c][rows, :] = got[:, c * LANES : (c + 1) * LANES]
            strips[3][rows, :B] = got[:, 3 * LANES :]
            pick(a)
        return carry

    lax.fori_loop(0, X_PARTS, some_planes, 0)
    for j in range(6):
        sends[j][GHOST_LEN:NEAR_AT, :] = extra
        out_copies.append(pltpu.make_async_copy(sends[j], outs[j], out_sem.at[j]))
        if j < 4:
            out_copies[-1].start()
    for r in range(SENT):
        if r < LAYERS * FAR:
            out, base = far, r * ROW_LEN
        elif r < LAYERS * FAR + NEAR:
            out, base = v4, NEAR_AT + (r - LAYERS * FAR) * ROW_LEN
        else:
            out, base = v5, NEAR_AT + (r - LAYERS * FAR - NEAR) * ROW_LEN
        got = [strip[pl.ds(r, B, stride=PITCH), :].astype(bf16) for strip in strips]
        for c in range(3):
            out[base + c * B : base + (c + 1) * B, :] = got[c]
        out[base + 3 * B : base + ROW_LEN, :] = jnp.concatenate(
            [got[3][:HALF, :B], got[3][HALF:, :B]], axis=1
        )
    out_copies.append(pltpu.make_async_copy(far, far_out, out_sem.at[7]))
    for copy in out_copies[5:]:
        copy.start()
    for copy in out_copies:
        copy.wait()


def pack(layer, lists, owner, touched, prolong, blocks):
    hbm = pl.BlockSpec(memory_space=pl.ANY)
    shapes = [(ROWS * HALF, LANES)] + [(n, LANES) for n in SEND_LEN]
    shapes += [(LAYERS * FAR * ROW_LEN, LANES)]
    return pl.pallas_call(
        pack_kernel,
        grid_spec=pltpu.PrefetchScalarGridSpec(
            num_scalar_prefetch=2,
            grid=(1,),
            in_specs=[
                pl.BlockSpec((1, ROWS), lambda i, *s: (0, 0)),
                pl.BlockSpec((1, U_DEV), lambda i, *s: (0, 0)),
                hbm,
                hbm,
            ],
            out_specs=[hbm] * 8,
            scratch_shapes=[pltpu.VMEM((ROWS, B * B), bf16)]
            + [pltpu.VMEM(shape, bf16) for shape in shapes]
            + [
                pltpu.VMEM((16 * PITCH, LANES), f32),
                pltpu.VMEM((B, NBR * B, ROWS), bf16),
            ]
            + [pltpu.VMEM((B * PITCH, LANES), f32)] * 4
            + [
                pltpu.SemaphoreType.DMA((P_PARTS,)),
                pltpu.SemaphoreType.DMA((X_PARTS,)),
                pltpu.SemaphoreType.DMA((8,)),
            ],
        ),
        out_shape=[jax.ShapeDtypeStruct(shape, bf16) for shape in shapes],
        compiler_params=pltpu.CompilerParams(vmem_limit_bytes=VMEM_LIMIT),
        cost_estimate=pl.CostEstimate(
            flops=2_000_000_000, transcendentals=0, bytes_accessed=23_000_000
        ),
        name="pack",
    )(layer, lists, owner, touched, prolong, blocks)


STEPS = 4
A_STEP = B // STEPS
R_STEP = ROWS // STEPS
TOTAL = ROWS
SPAN = TOTAL + 1


def left_kernel(arrival, blocks, halves, left, table0, table1, transposed, picks):
    j, step = pl.program_id(0), pl.program_id(1)
    tables = (table0, table1)
    square = (ROWS, ROWS)

    @pl.when((j == 0) & (step == 0))
    def _():
        wide = (LANES, LANES)
        eye = lax.broadcasted_iota(jnp.int32, wide, 0) == lax.broadcasted_iota(jnp.int32, wide, 1)
        eye = eye.astype(f32).astype(bf16)

        def turn(n, carry):
            tiles = halves[pl.ds(pl.multiple_of(n * 8 * HALF, 8 * HALF), 8 * HALF), :]
            got = lax.dot_general(eye, tiles, NT, preferred_element_type=f32).astype(bf16)
            for g in range(2):
                lanes = slice(g * LANES, (g + 1) * LANES)
                transposed[2 * n + g] = jnp.concatenate([got[:B, lanes], got[B:, lanes]], axis=1)
            return carry

        lax.fori_loop(0, ROWS // 8, turn, 0, unroll=8)

        down_rows = lax.broadcasted_iota(jnp.int32, square, 0)
        along = lax.broadcasted_iota(jnp.int32, square, 1)
        taken = (down_rows == arrival[...]).astype(f32).astype(bf16)
        unit = (down_rows == along).astype(f32).astype(bf16)
        picks[...] = lax.dot_general(unit, taken, NT, preferred_element_type=f32).astype(bf16)

    def relay(width):
        def plane(n, carry):
            rows = pl.ds((step * A_STEP + n) * SPAN, TOTAL)
            got = lax.dot_general(
                picks[...], blocks[n, :width], NT, preferred_element_type=f32
            )
            table0[rows, :] = got[:, :LANES]
            table1[rows, : width - LANES] = got[:, LANES:]
            return carry

        lax.fori_loop(0, A_STEP, plane, 0, unroll=16)

    @pl.when((step < STEPS) & (j == 0))
    def _():
        relay(2 * LANES)

    @pl.when((step < STEPS) & (j == 1))
    def _():
        relay(LANES + B)

    whose = lax.broadcasted_iota(jnp.int32, (B, 2 * LANES), 1) % LANES // HALF

    def four(n):
        i = (step - STEPS) * R_STEP + 4 * n
        rows = [
            jnp.concatenate(
                [t[pl.ds(i + q, B, stride=SPAN), :].astype(bf16) for t in tables], axis=1
            )
            for q in range(4)
        ]
        weights = jnp.concatenate([r[:HALF] for r in rows] + [r[HALF:] for r in rows], axis=0)
        base = transposed[(step - STEPS) * (R_STEP // 4) + n]
        mine = [jnp.where(whose == q, base, jnp.zeros((), bf16)) for q in range(4)]
        got = jnp.dot(jnp.concatenate(mine, axis=0), weights, preferred_element_type=f32)
        return [got[q * B : (q + 1) * B].astype(bf16) for q in range(4)]

    @pl.when((step >= STEPS) & (j == 0))
    def _():
        def multiply(n, carry):
            for q, part in enumerate(four(n)):
                left[0, 4 * n + q] = part[:, :LANES]
                left[1, 4 * n + q] = part[:, LANES:]
            return carry

        lax.fori_loop(0, R_STEP // 4, multiply, 0, unroll=16)

    @pl.when((step >= STEPS) & (j == 1))
    def _():
        def multiply(n, carry):
            parts = four(n)
            for q in range(4):
                left[0, 4 * n + q] = parts[q][:, :LANES]
            for h in range(2):
                left[1, 2 * n + h] = jnp.concatenate(
                    [p[:, LANES : LANES + B] for p in parts[2 * h : 2 * h + 2]], axis=1
                )
            return carry

        lax.fori_loop(0, R_STEP // 4, multiply, 0, unroll=16)


def make_left(arrival, blocks, halves):
    whole = lambda shape: pl.BlockSpec(shape, lambda j, s: (0,) * len(shape))
    return pl.pallas_call(
        left_kernel,
        grid=(2, 2 * STEPS),
        in_specs=[
            whole((1, ROWS)),
            pl.BlockSpec(
                (A_STEP, 2 * LANES, ROWS), lambda j, s: (jnp.minimum(s, STEPS - 1), j, 0)
            ),
            whole((ROWS * HALF, LANES)),
        ],
        out_specs=pl.BlockSpec(
            (2, R_STEP, B, LANES), lambda j, s: (j, jnp.maximum(s - STEPS, 0), 0, 0)
        ),
        out_shape=jax.ShapeDtypeStruct((4, ROWS, B, LANES), bf16),
        scratch_shapes=[
            pltpu.VMEM((B * SPAN, LANES), f32),
            pltpu.VMEM((B * SPAN, LANES), f32),
            pltpu.VMEM((ROWS // 4, B, 2 * LANES), bf16),
            pltpu.VMEM((ROWS, ROWS), bf16),
        ],
        compiler_params=pltpu.CompilerParams(
            vmem_limit_bytes=VMEM_LIMIT, dimension_semantics=("arbitrary", "arbitrary")
        ),
        cost_estimate=pl.CostEstimate(
            flops=12_000_000_000, transcendentals=0, bytes_accessed=60_000_000
        ),
        name="left",
    )(arrival, blocks, halves)


PARTS = 8
TALL = B + 1


def sums_kernel(
    moved_rows, columns, targets, left_hbm, halves, g0, g1, g2, g3, g4, g5, far,
    own, fine, s0, s1, s2, s3, s4, s5,
    left, packed, acc0, acc1, moved, left_sem, table_sem, moved_sem,
):
    ghosts = (g0, g1, g2, g3, g4, g5)
    sends = (s0, s1, s2, s3, s4, s5)
    totals = (acc0, acc1)
    part = ROWS // PARTS
    table_copies = [pltpu.make_async_copy(halves, packed.at[: ROWS * HALF, :], table_sem.at[0])]
    for j in range(6):
        first = (ROWS + j * GCAP) * HALF
        table_copies.append(
            pltpu.make_async_copy(
                ghosts[j].at[:GHOST_LEN, :],
                packed.at[first : first + GHOST_LEN, :],
                table_sem.at[1 + j],
            )
        )
    first, second = LAYERS * FAR * ROW_LEN, (LAYERS * FAR + NEAR) * ROW_LEN
    moved_copies = [
        pltpu.make_async_copy(far, moved.at[:first, :], moved_sem.at[0]),
        pltpu.make_async_copy(g5.at[NEAR_AT:, :], moved.at[first:second, :], moved_sem.at[1]),
        pltpu.make_async_copy(g4.at[NEAR_AT:, :], moved.at[second:, :], moved_sem.at[2]),
    ]

    def left_copy(n):
        rows = pl.ds(n * part, part)
        return pltpu.make_async_copy(left_hbm.at[:, rows], left.at[:, rows], left_sem.at[n])

    for copy in table_copies + moved_copies:
        copy.start()
    for n in range(PARTS):
        left_copy(n).start()

    def clear(u, carry):
        for total in totals:
            total[pl.ds(u * TALL, TALL), :] = jnp.zeros((TALL, LANES), f32)
        return carry

    lax.fori_loop(0, U_DEV + 1, clear, 0, unroll=5)

    def tile(c):
        return packed[pl.ds(pl.multiple_of(c * HALF, HALF), HALF), :]

    def beside(p, q):
        return jnp.concatenate(
            [
                jnp.concatenate([p[:, :B], q[:, :B]], axis=1),
                jnp.concatenate([p[:, B:], q[:, B:]], axis=1),
            ],
            axis=0,
        )

    for copy in table_copies + moved_copies:
        copy.wait()

    def arrive(m, carry):
        last = []
        for s in (2 * m, 2 * m + 1):
            own_tile = tile(jnp.maximum(moved_rows[0, s], 0))
            block = jnp.concatenate([own_tile[:, :B], own_tile[:, B:]], axis=0)
            base = pl.multiple_of(s * ROW_LEN, HALF)
            h = moved[pl.ds(base + 3 * B, HALF), :]
            chunks = [moved[pl.ds(base + c * B, B), :] for c in range(3)]
            chunks.append(jnp.concatenate([h[:, :B], h[:, B:]], axis=0))
            got = lax.dot_general(
                block, jnp.concatenate(chunks, axis=1), (((0,), (0,)), ((), ())),
                preferred_element_type=f32,
            ).astype(bf16)
            for c in range(3):
                left[c, ROWS + s] = got[:, c * LANES : (c + 1) * LANES]
            last.append(got[:, 3 * LANES :])
        left[3, ROWS + m] = jnp.concatenate(last, axis=1)
        return carry

    lax.fori_loop(0, SENT // 2, arrive, 0, unroll=6)

    zero = jnp.zeros((B, LANES), bf16)

    def quad(a, b, entries):
        slots = [slot for slot, _ in entries]
        tiles = [tile(col) for _, col in entries]
        weights = jnp.concatenate(
            [
                jnp.concatenate([beside(tiles[0], tiles[2]), zero], axis=1),
                jnp.concatenate([zero, beside(tiles[1], tiles[3])], axis=1),
            ],
            axis=0,
        )
        rows = jnp.concatenate([a, b], axis=0)
        got = jnp.dot(rows, weights, preferred_element_type=f32)
        for side in range(2):
            for part in range(2):
                first = side * LANES + part * B
                lanes = slice(part * B, (part + 1) * B)
                value = got[part * B : (part + 1) * B, first : first + B]
                totals[side][pl.ds(slots[side + 2 * part] * TALL, B), lanes] += value

    def four_rows(i, pair, sources):
        entries = []
        for n, valid in sources:
            cols = [columns[k, n] for k in range(NBR)]
            entries.append(
                [
                    (
                        jnp.where((cols[k] >= 0) & valid, targets[k, n], U_DEV),
                        jnp.maximum(cols[k], 0),
                    )
                    for k in range(NBR)
                ]
            )
        for r in range(4):
            quad(left[0, i + r], left[1, i + r], entries[r][:4])
        for r in (0, 2):
            quad(left[2, i + r], left[2, i + r + 1], entries[r][4:6] + entries[r + 1][4:6])
        quad(left[3, pair], left[3, pair + 1], [e[6] for e in entries])

    def one_part(n, carry):
        left_copy(n).wait()
        for m in range(part // 4):
            i = n * part + 4 * m
            pair = (n >> 1) * R_STEP + (n & 1) * (part // 2) + 2 * m
            four_rows(i, pair, [(i + r, True) for r in range(4)])
        return carry

    lax.fori_loop(0, PARTS, one_part, 0)
    for s in range(0, SENT, 4):
        sources = [moved_rows[0, s + r] for r in range(4)]
        four_rows(
            ROWS + s, ROWS + s // 2, [(jnp.maximum(n, 0), n >= 0) for n in sources]
        )
    low = lower_lanes((16, LANES))

    def summed(u, b):
        rows = [pl.ds((u + 8 * n) * TALL + b, 8, stride=TALL) for n in range(2)]
        return jnp.concatenate([acc0[r, :] + acc1[r, :] for r in rows], axis=0)

    for v in range(7):
        for half in range(2):
            u, at = v * UCAP + half * 16, slice(half * 16, half * 16 + 16)

            def gather(s, carry):
                a, b = summed(u, 2 * s), summed(u, 2 * s + 1)
                value = jnp.where(low, a, b) + pltpu.roll(jnp.where(low, b, a), B, 1)
                lanes = pl.ds(pl.multiple_of(s * LANES, LANES), LANES)
                coarse = value.astype(bf16)
                if v == 0:
                    own[at, lanes] = coarse
                    fine[at, lanes] = (value - coarse.astype(f32)).astype(bf16)
                else:
                    sends[v - 1][at, lanes] = coarse
                return carry

            lax.fori_loop(0, HALF, gather, 0, unroll=32)


def make_sums(moved_rows, columns, targets, left, halves, ghosts, far):
    hbm = pl.BlockSpec(memory_space=pl.ANY)
    return pl.pallas_call(
        sums_kernel,
        grid_spec=pltpu.PrefetchScalarGridSpec(
            num_scalar_prefetch=3,
            grid=(1,),
            in_specs=[hbm] * 9,
            out_specs=[pl.BlockSpec((UCAP, B * B), lambda i, *s: (0, 0))] * 8,
            scratch_shapes=[
                pltpu.VMEM((4, ROWS + SENT, B, LANES), bf16),
                pltpu.VMEM((TABLE * HALF, LANES), bf16),
            ]
            + [pltpu.VMEM(((U_DEV + 1) * TALL, LANES), f32)] * 2
            + [
                pltpu.VMEM((SENT * ROW_LEN, LANES), bf16),
                pltpu.SemaphoreType.DMA((PARTS,)),
                pltpu.SemaphoreType.DMA((7,)),
                pltpu.SemaphoreType.DMA((3,)),
            ],
        ),
        out_shape=[jax.ShapeDtypeStruct((UCAP, B * B), bf16)] * 8,
        compiler_params=pltpu.CompilerParams(vmem_limit_bytes=VMEM_LIMIT),
        cost_estimate=pl.CostEstimate(
            flops=8_000_000_000, transcendentals=0, bytes_accessed=30_000_000
        ),
        name="sums",
    )(moved_rows, columns, targets, left, halves, *ghosts, far)


def final_kernel(
    touched, own, fine, r0, r1, r2, r3, r4, r5, g0, g1, g2, g3, g4, g5, out,
    stack, numbers, sem, number_sem,
):
    parts = (own, r0, r1, r2, r3, r4, r5, fine)
    ghosts = (g0, g1, g2, g3, g4, g5)
    copies = [
        pltpu.make_async_copy(
            ghosts[f ^ 1].at[GHOST_LEN:NEAR_AT, :], numbers.at[f], number_sem.at[f]
        )
        for f in range(6)
    ]
    copies += [
        pltpu.make_async_copy(parts[v], stack.at[v * UCAP : (v + 1) * UCAP, :], sem.at[v])
        for v in range(8)
    ]
    for copy in copies:
        copy.start()
    lane = lax.broadcasted_iota(jnp.int32, (1, LANES), 1) // UCAP
    wide = touched[...]
    for copy in copies:
        copy.wait()
    given = [numbers[f].astype(f32) for f in range(6)]
    first = wide[:, :LANES].astype(f32)
    for f in range(3):
        first = jnp.where(lane == f + 1, given[f][0:1, :], first)
    second = jnp.concatenate([wide[:, :UCAP]] * 4, axis=1).astype(f32)
    for f in range(3, 6):
        second = jnp.where(lane == f - 3, given[f][1:2, :], second)
    row = lax.broadcasted_iota(jnp.int32, (CE_DEV, LANES), 0).astype(f32)
    select = jnp.concatenate(
        [(row == first).astype(f32), (row == second).astype(f32)], axis=1
    ).astype(bf16)
    for n in range(8):
        lanes = slice(n * 4 * LANES, (n + 1) * 4 * LANES)
        out[:, lanes] = jnp.dot(select, stack[:, lanes], preferred_element_type=f32)


def make_final(touched, own, fine, got, ghosts):
    hbm = pl.BlockSpec(memory_space=pl.ANY)
    return pl.pallas_call(
        final_kernel,
        grid=(1,),
        in_specs=[pl.BlockSpec((1, U_DEV), lambda i: (0, 0))] + [hbm] * 14,
        out_specs=pl.BlockSpec((CE_DEV, B * B), lambda i: (0, 0)),
        scratch_shapes=[
            pltpu.VMEM((8 * UCAP, B * B), bf16),
            pltpu.VMEM((6, EXTRA, LANES), bf16),
            pltpu.SemaphoreType.DMA((8,)),
            pltpu.SemaphoreType.DMA((6,)),
        ],
        out_shape=jax.ShapeDtypeStruct((CE_DEV, B * B), f32),
        compiler_params=pltpu.CompilerParams(vmem_limit_bytes=VMEM_LIMIT),
        name="final",
    )(touched, own, fine, *got, *ghosts)


def neighbour_shift(value, facing):
    axis = AXES[facing // 2]
    return shifted(value, axis, 1 - 2 * (facing % 2))


def one_shard(blocks, prolong, new_owner, arrival, columns, targets, ghost_lists, touched):
    own_layer = lax.axis_index("gz")
    planes = jnp.transpose(blocks, (1, 2, 0))
    halves, *outbound, far = pack(
        own_layer[None], jnp.transpose(ghost_lists, (1, 0, 2)), new_owner[None], touched,
        prolong, planes,
    )
    ghosts = []
    for facing in range(6):
        ghosts.append(neighbour_shift(outbound[facing ^ 1], facing ^ 1))
    far_in = lax.all_to_all(
        far.reshape(LAYERS, FAR * ROW_LEN, LANES), "gz", split_axis=0, concat_axis=0, tiled=True
    )
    left = make_left(arrival[None], planes, halves)

    old = jnp.arange(ROWS, dtype=jnp.int32)
    labels = jnp.arange(LAYERS, dtype=jnp.int32)
    ranks = jnp.arange(FAR, dtype=jnp.int32)
    later = FAR + jnp.arange(NEAR, dtype=jnp.int32)
    codes = ROWS + jnp.concatenate(
        [
            (labels[:, None] * CAP + ranks[None, :]).reshape(-1),
            (own_layer - 1) * CAP + later,
            (own_layer + 1) * CAP + later,
        ]
    )
    match = (codes[:, None] == arrival[None, :]) & (codes[:, None] >= ROWS)
    row_of = jnp.sum(jnp.where(match, old[None, :] + 1, 0), axis=1) - 1
    own, fine, *sends = make_sums(
        row_of[None, :], columns.T, targets.T, left, halves, ghosts,
        far_in.reshape(LAYERS * FAR * ROW_LEN, LANES),
    )
    got = [neighbour_shift(sends[facing], facing) for facing in range(6)]
    return make_final(touched, own, fine, got, ghosts)


def solution(mesh):
    return jax.shard_map(
        one_shard,
        mesh=mesh,
        in_specs=(
            P(AXES, None, None),
            P(AXES, None),
            P(AXES),
            P(AXES),
            P(AXES, None),
            P(AXES, None),
            P(AXES, None, None),
            P(AXES, None),
        ),
        out_specs=P(AXES, None),
        check_vma=False,
    )
```

```python
import jax
import jax.numpy as jnp
from jax import lax
from jax.experimental import pallas as pl
from jax.experimental.pallas import tpu as pltpu
from jax.sharding import PartitionSpec as P


B = 64
NBR = 7
CAP = 6
FAR = 2
NEAR = CAP - FAR
GCAP = 64
UCAP = 32
U_DEV = 224
CE_DEV = 64
ROWS = 256
LAYERS = 8
HALF = 32
LANES = 128
AXES = ("gx", "gy", "gz")
SENT = LAYERS * FAR + 2 * NEAR
SENT_PAD = 32
ROW_LEN = 3 * B + HALF
GHOST_LEN = GCAP * HALF
EXTRA = 16
TABLE = ROWS + 6 * GCAP
VMEM_LIMIT = 62 * 1024 * 1024
PITCH = HALF + 1
bf16 = jnp.bfloat16
f32 = jnp.float32


def lower_lanes(shape):
    return lax.broadcasted_iota(jnp.int32, shape, len(shape) - 1) < B


def shifted(value, axis, by):
    devices = lax.axis_size(axis)
    pairs = [(i, i + by) for i in range(devices) if 0 <= i + by < devices]
    return lax.ppermute(value, axis, pairs)


NEAR_AT = GHOST_LEN + EXTRA
SEND_LEN = [NEAR_AT] * 4 + [NEAR_AT + NEAR * ROW_LEN] * 2
P_PARTS = 4
X_PARTS = 8
NT = (((1,), (1,)), ((), ()))


def pack_kernel(
    layer, lists, owner, touched, prolong_hbm, blocks, halves_out, o0, o1, o2, o3, o4, o5, far_out,
    prolong, halves, v0, v1, v2, v3, v4, v5, far, work, planes, strip0, strip1, strip2, strip3,
    in_sem, plane_sem, out_sem,
):
    sends, outs = (v0, v1, v2, v3, v4, v5), (o0, o1, o2, o3, o4, o5)
    strips = (strip0, strip1, strip2, strip3)
    count, deep = ROWS // P_PARTS, B // X_PARTS

    def prolong_copy(n):
        rows = pl.ds(n * count, count)
        return pltpu.make_async_copy(prolong_hbm.at[rows], prolong.at[rows], in_sem.at[n])

    def plane_copy(n):
        some = pl.ds(n * deep, deep)
        return pltpu.make_async_copy(blocks.at[some], planes.at[some], plane_sem.at[n])

    for n in range(P_PARTS):
        prolong_copy(n).start()
    square = (ROWS, ROWS)
    peer = lax.rem(owner[...], LAYERS)
    member = lax.broadcasted_iota(jnp.int32, (16, ROWS), 0) == peer
    earlier = (
        lax.broadcasted_iota(jnp.int32, square, 0) < lax.broadcasted_iota(jnp.int32, square, 1)
    )
    before = jnp.dot(
        member.astype(f32).astype(bf16),
        earlier.astype(f32).astype(bf16),
        preferred_element_type=f32,
    )
    rank = jnp.sum(jnp.where(member, before, 0.0), axis=0, keepdims=True).astype(jnp.int32)
    near_slot = jnp.where(peer > layer[0], LAYERS * FAR, LAYERS * FAR + NEAR) + rank - FAR
    slot = jnp.where(rank < FAR, peer * FAR + rank, near_slot)
    slot = jnp.where(peer == layer[0], -1, slot)
    sent = lax.broadcasted_iota(jnp.int32, (SENT_PAD, ROWS), 0) == slot
    picks = sent.astype(f32).astype(bf16)

    low = lower_lanes((16, LANES))

    def group(g, carry):
        rows = pl.ds(pl.multiple_of(g * 16, 16), 16)
        for s in range(16):
            near = prolong[rows, s * LANES : (s + 1) * LANES].astype(f32)
            far_half = prolong[rows, (s + 16) * LANES : (s + 17) * LANES].astype(f32)
            even = jnp.where(low, near, pltpu.roll(far_half, B, 1))
            odd = jnp.where(low, pltpu.roll(near, B, 1), far_half)
            work[pl.ds(2 * s, 16, stride=PITCH), :] = even
            work[pl.ds(2 * s + 1, 16, stride=PITCH), :] = odd
        for e in range(16):
            halves[pl.ds(pl.multiple_of((g * 16 + e) * HALF, HALF), HALF), :] = work[
                e * PITCH : e * PITCH + HALF, :
            ].astype(bf16)
        return carry

    for n in range(P_PARTS):
        prolong_copy(n).wait()
        if n == 0:
            for m in range(X_PARTS):
                plane_copy(m).start()
        lax.fori_loop(n * count // 16, (n + 1) * count // 16, group, 0)
    out_copies = [pltpu.make_async_copy(halves, halves_out, out_sem.at[6])]
    out_copies[0].start()

    top = touched[:, :LANES]
    rest = jnp.concatenate(
        [touched[:, LANES:], jnp.zeros((1, 2 * LANES - U_DEV), jnp.int32)], axis=1
    )
    at = lax.broadcasted_iota(jnp.int32, (EXTRA, LANES), 0)
    extra = jnp.where(at == 0, top, jnp.where(at == 1, rest, 0)).astype(f32).astype(bf16)

    def pick(q):
        for j in range(6):
            row = lists[j, 0, q]
            sends[j][pl.ds(pl.multiple_of(q * HALF, HALF), HALF), :] = halves[
                pl.ds(pl.multiple_of(row * HALF, HALF), HALF), :
            ]

    def some_planes(n, carry):
        plane_copy(n).wait()
        for d in range(deep):
            a = n * deep + d
            got = lax.dot_general(picks, planes[a], NT, preferred_element_type=f32)
            rows = pl.ds(a * PITCH, SENT_PAD)
            for c in range(3):
                strips[c][rows, :] = got[:, c * LANES : (c + 1) * LANES]
            strips[3][rows, :B] = got[:, 3 * LANES :]
            pick(a)
        return carry

    lax.fori_loop(0, X_PARTS, some_planes, 0)
    for j in range(6):
        sends[j][GHOST_LEN:NEAR_AT, :] = extra
        some = pl.ds(0, NEAR_AT)
        out_copies.append(
            pltpu.make_async_copy(sends[j].at[some], outs[j].at[some], out_sem.at[j])
        )
        out_copies[-1].start()
    for r in range(SENT):
        if r < LAYERS * FAR:
            out, base = far, r * ROW_LEN
        elif r < LAYERS * FAR + NEAR:
            out, base = v4, NEAR_AT + (r - LAYERS * FAR) * ROW_LEN
        else:
            out, base = v5, NEAR_AT + (r - LAYERS * FAR - NEAR) * ROW_LEN
        got = [strip[pl.ds(r, B, stride=PITCH), :].astype(bf16) for strip in strips]
        for c in range(3):
            out[base + c * B : base + (c + 1) * B, :] = got[c]
        out[base + 3 * B : base + ROW_LEN, :] = jnp.concatenate(
            [got[3][:HALF, :B], got[3][HALF:, :B]], axis=1
        )
    late_copies = [pltpu.make_async_copy(far, far_out, out_sem.at[7])]
    for j in (4, 5):
        some = pl.ds(NEAR_AT, NEAR * ROW_LEN)
        late_copies.append(
            pltpu.make_async_copy(sends[j].at[some], outs[j].at[some], out_sem.at[j + 4])
        )
    for copy in late_copies:
        copy.start()
    out_copies += late_copies
    for copy in out_copies:
        copy.wait()


def pack(layer, lists, owner, touched, prolong, blocks):
    hbm = pl.BlockSpec(memory_space=pl.ANY)
    shapes = [(ROWS * HALF, LANES)] + [(n, LANES) for n in SEND_LEN]
    shapes += [(LAYERS * FAR * ROW_LEN, LANES)]
    return pl.pallas_call(
        pack_kernel,
        grid_spec=pltpu.PrefetchScalarGridSpec(
            num_scalar_prefetch=2,
            grid=(1,),
            in_specs=[
                pl.BlockSpec((1, ROWS), lambda i, *s: (0, 0)),
                pl.BlockSpec((1, U_DEV), lambda i, *s: (0, 0)),
                hbm,
                hbm,
            ],
            out_specs=[hbm] * 8,
            scratch_shapes=[pltpu.VMEM((ROWS, B * B), bf16)]
            + [pltpu.VMEM(shape, bf16) for shape in shapes]
            + [
                pltpu.VMEM((16 * PITCH, LANES), f32),
                pltpu.VMEM((B, NBR * B, ROWS), bf16),
            ]
            + [pltpu.VMEM((B * PITCH, LANES), f32)] * 4
            + [
                pltpu.SemaphoreType.DMA((P_PARTS,)),
                pltpu.SemaphoreType.DMA((X_PARTS,)),
                pltpu.SemaphoreType.DMA((10,)),
            ],
        ),
        out_shape=[jax.ShapeDtypeStruct(shape, bf16) for shape in shapes],
        compiler_params=pltpu.CompilerParams(vmem_limit_bytes=VMEM_LIMIT),
        cost_estimate=pl.CostEstimate(
            flops=2_000_000_000, transcendentals=0, bytes_accessed=23_000_000
        ),
        name="pack",
    )(layer, lists, owner, touched, prolong, blocks)


STEPS = 4
A_STEP = B // STEPS
R_STEP = ROWS // STEPS
TOTAL = ROWS
SPAN = TOTAL + 1


def left_kernel(arrival, blocks, halves, left, table0, table1, transposed, picks):
    j, step = pl.program_id(0), pl.program_id(1)
    tables = (table0, table1)
    square = (ROWS, ROWS)

    @pl.when((j == 0) & (step == 0))
    def _():
        wide = (LANES, LANES)
        eye = lax.broadcasted_iota(jnp.int32, wide, 0) == lax.broadcasted_iota(jnp.int32, wide, 1)
        eye = eye.astype(f32).astype(bf16)

        def turn(n, carry):
            tiles = halves[pl.ds(pl.multiple_of(n * 8 * HALF, 8 * HALF), 8 * HALF), :]
            got = lax.dot_general(eye, tiles, NT, preferred_element_type=f32).astype(bf16)
            for g in range(2):
                lanes = slice(g * LANES, (g + 1) * LANES)
                transposed[2 * n + g] = jnp.concatenate([got[:B, lanes], got[B:, lanes]], axis=1)
            return carry

        lax.fori_loop(0, ROWS // 8, turn, 0, unroll=8)

        down_rows = lax.broadcasted_iota(jnp.int32, square, 0)
        along = lax.broadcasted_iota(jnp.int32, square, 1)
        taken = (down_rows == arrival[...]).astype(f32).astype(bf16)
        unit = (down_rows == along).astype(f32).astype(bf16)
        picks[...] = lax.dot_general(unit, taken, NT, preferred_element_type=f32).astype(bf16)

    def relay(width):
        def plane(n, carry):
            rows = pl.ds((step * A_STEP + n) * SPAN, TOTAL)
            got = lax.dot_general(
                picks[...], blocks[n, :width], NT, preferred_element_type=f32
            )
            table0[rows, :] = got[:, :LANES]
            table1[rows, : width - LANES] = got[:, LANES:]
            return carry

        lax.fori_loop(0, A_STEP, plane, 0, unroll=16)

    @pl.when((step < STEPS) & (j == 0))
    def _():
        relay(2 * LANES)

    @pl.when((step < STEPS) & (j == 1))
    def _():
        relay(LANES + B)

    whose = lax.broadcasted_iota(jnp.int32, (B, 2 * LANES), 1) % LANES // HALF

    def four(n):
        i = (step - STEPS) * R_STEP + 4 * n
        rows = [
            jnp.concatenate(
                [t[pl.ds(i + q, B, stride=SPAN), :].astype(bf16) for t in tables], axis=1
            )
            for q in range(4)
        ]
        weights = jnp.concatenate([r[:HALF] for r in rows] + [r[HALF:] for r in rows], axis=0)
        base = transposed[(step - STEPS) * (R_STEP // 4) + n]
        mine = [jnp.where(whose == q, base, jnp.zeros((), bf16)) for q in range(4)]
        got = jnp.dot(jnp.concatenate(mine, axis=0), weights, preferred_element_type=f32)
        return [got[q * B : (q + 1) * B].astype(bf16) for q in range(4)]

    @pl.when((step >= STEPS) & (j == 0))
    def _():
        def multiply(n, carry):
            for q, part in enumerate(four(n)):
                left[0, 4 * n + q] = part[:, :LANES]
                left[1, 4 * n + q] = part[:, LANES:]
            return carry

        lax.fori_loop(0, R_STEP // 4, multiply, 0, unroll=16)

    @pl.when((step >= STEPS) & (j == 1))
    def _():
        def multiply(n, carry):
            parts = four(n)
            for q in range(4):
                left[0, 4 * n + q] = parts[q][:, :LANES]
            for h in range(2):
                left[1, 2 * n + h] = jnp.concatenate(
                    [p[:, LANES : LANES + B] for p in parts[2 * h : 2 * h + 2]], axis=1
                )
            return carry

        lax.fori_loop(0, R_STEP // 4, multiply, 0, unroll=16)


def make_left(arrival, blocks, halves):
    whole = lambda shape: pl.BlockSpec(shape, lambda j, s: (0,) * len(shape))
    return pl.pallas_call(
        left_kernel,
        grid=(2, 2 * STEPS),
        in_specs=[
            whole((1, ROWS)),
            pl.BlockSpec(
                (A_STEP, 2 * LANES, ROWS), lambda j, s: (jnp.minimum(s, STEPS - 1), j, 0)
            ),
            whole((ROWS * HALF, LANES)),
        ],
        out_specs=pl.BlockSpec(
            (2, R_STEP, B, LANES), lambda j, s: (j, jnp.maximum(s - STEPS, 0), 0, 0)
        ),
        out_shape=jax.ShapeDtypeStruct((4, ROWS, B, LANES), bf16),
        scratch_shapes=[
            pltpu.VMEM((B * SPAN, LANES), f32),
            pltpu.VMEM((B * SPAN, LANES), f32),
            pltpu.VMEM((ROWS // 4, B, 2 * LANES), bf16),
            pltpu.VMEM((ROWS, ROWS), bf16),
        ],
        compiler_params=pltpu.CompilerParams(
            vmem_limit_bytes=VMEM_LIMIT, dimension_semantics=("arbitrary", "arbitrary")
        ),
        cost_estimate=pl.CostEstimate(
            flops=12_000_000_000, transcendentals=0, bytes_accessed=60_000_000
        ),
        name="left",
    )(arrival, blocks, halves)


PARTS = 4
TALL = B + 1


def sums_kernel(
    moved_rows, columns, targets, left_hbm, halves, g0, g1, g2, g3, g4, g5, far,
    own, fine, s0, s1, s2, s3, s4, s5,
    left, packed, acc0, acc1, moved, left_sem, table_sem, moved_sem,
):
    ghosts = (g0, g1, g2, g3, g4, g5)
    sends = (s0, s1, s2, s3, s4, s5)
    totals = (acc0, acc1)
    part = ROWS // PARTS
    table_copies = [pltpu.make_async_copy(halves, packed.at[: ROWS * HALF, :], table_sem.at[0])]
    for j in range(6):
        first = (ROWS + j * GCAP) * HALF
        table_copies.append(
            pltpu.make_async_copy(
                ghosts[j].at[:GHOST_LEN, :],
                packed.at[first : first + GHOST_LEN, :],
                table_sem.at[1 + j],
            )
        )
    first, second = LAYERS * FAR * ROW_LEN, (LAYERS * FAR + NEAR) * ROW_LEN
    moved_copies = [
        pltpu.make_async_copy(far, moved.at[:first, :], moved_sem.at[0]),
        pltpu.make_async_copy(g5.at[NEAR_AT:, :], moved.at[first:second, :], moved_sem.at[1]),
        pltpu.make_async_copy(g4.at[NEAR_AT:, :], moved.at[second:, :], moved_sem.at[2]),
    ]

    def left_copy(n):
        rows = pl.ds(n * part, part)
        return pltpu.make_async_copy(left_hbm.at[:, rows], left.at[:, rows], left_sem.at[n])

    for copy in table_copies + moved_copies:
        copy.start()
    for n in range(PARTS):
        left_copy(n).start()

    def clear(u, carry):
        for total in totals:
            total[pl.ds(u * TALL, TALL), :] = jnp.zeros((TALL, LANES), f32)
        return carry

    lax.fori_loop(0, U_DEV + 1, clear, 0, unroll=5)

    def tile(c):
        return packed[pl.ds(pl.multiple_of(c * HALF, HALF), HALF), :]

    def beside(p, q):
        return jnp.concatenate(
            [
                jnp.concatenate([p[:, :B], q[:, :B]], axis=1),
                jnp.concatenate([p[:, B:], q[:, B:]], axis=1),
            ],
            axis=0,
        )

    for copy in table_copies + moved_copies:
        copy.wait()

    def arrive(m, carry):
        last = []
        for s in (2 * m, 2 * m + 1):
            own_tile = tile(jnp.maximum(moved_rows[0, s], 0))
            block = jnp.concatenate([own_tile[:, :B], own_tile[:, B:]], axis=0)
            base = pl.multiple_of(s * ROW_LEN, HALF)
            h = moved[pl.ds(base + 3 * B, HALF), :]
            chunks = [moved[pl.ds(base + c * B, B), :] for c in range(3)]
            chunks.append(jnp.concatenate([h[:, :B], h[:, B:]], axis=0))
            got = lax.dot_general(
                block, jnp.concatenate(chunks, axis=1), (((0,), (0,)), ((), ())),
                preferred_element_type=f32,
            ).astype(bf16)
            for c in range(3):
                left[c, ROWS + s] = got[:, c * LANES : (c + 1) * LANES]
            last.append(got[:, 3 * LANES :])
        left[3, ROWS + m] = jnp.concatenate(last, axis=1)
        return carry

    lax.fori_loop(0, SENT // 2, arrive, 0, unroll=6)

    zero = jnp.zeros((B, LANES), bf16)

    def quad(a, b, entries):
        slots = [slot for slot, _ in entries]
        tiles = [tile(col) for _, col in entries]
        weights = jnp.concatenate(
            [
                jnp.concatenate([beside(tiles[0], tiles[2]), zero], axis=1),
                jnp.concatenate([zero, beside(tiles[1], tiles[3])], axis=1),
            ],
            axis=0,
        )
        rows = jnp.concatenate([a, b], axis=0)
        got = jnp.dot(rows, weights, preferred_element_type=f32)
        for side in range(2):
            for part in range(2):
                first = side * LANES + part * B
                lanes = slice(part * B, (part + 1) * B)
                value = got[part * B : (part + 1) * B, first : first + B]
                totals[side][pl.ds(slots[side + 2 * part] * TALL, B), lanes] += value

    def four_rows(i, pair, sources):
        entries = []
        for n, valid in sources:
            cols = [columns[k, n] for k in range(NBR)]
            entries.append(
                [
                    (
                        jnp.where((cols[k] >= 0) & valid, targets[k, n], U_DEV),
                        jnp.maximum(cols[k], 0),
                    )
                    for k in range(NBR)
                ]
            )
        for r in range(4):
            quad(left[0, i + r], left[1, i + r], entries[r][:4])
        for r in (0, 2):
            quad(left[2, i + r], left[2, i + r + 1], entries[r][4:6] + entries[r + 1][4:6])
        quad(left[3, pair], left[3, pair + 1], [e[6] for e in entries])

    def one_part(n, carry):
        left_copy(n).wait()
        for m in range(part // 4):
            i = n * part + 4 * m
            pair = n * part + 2 * m
            four_rows(i, pair, [(i + r, True) for r in range(4)])
        return carry

    lax.fori_loop(0, PARTS, one_part, 0)
    for s in range(0, SENT, 4):
        sources = [moved_rows[0, s + r] for r in range(4)]
        four_rows(
            ROWS + s, ROWS + s // 2, [(jnp.maximum(n, 0), n >= 0) for n in sources]
        )
    low = lower_lanes((16, LANES))

    def summed(u, b):
        rows = [pl.ds((u + 8 * n) * TALL + b, 8, stride=TALL) for n in range(2)]
        return jnp.concatenate([acc0[r, :] + acc1[r, :] for r in rows], axis=0)

    for v in range(7):
        for half in range(2):
            u, at = v * UCAP + half * 16, slice(half * 16, half * 16 + 16)

            def gather(s, carry):
                a, b = summed(u, 2 * s), summed(u, 2 * s + 1)
                value = jnp.where(low, a, b) + pltpu.roll(jnp.where(low, b, a), B, 1)
                lanes = pl.ds(pl.multiple_of(s * LANES, LANES), LANES)
                coarse = value.astype(bf16)
                if v == 0:
                    own[at, lanes] = coarse
                    fine[at, lanes] = (value - coarse.astype(f32)).astype(bf16)
                else:
                    sends[v - 1][at, lanes] = coarse
                return carry

            lax.fori_loop(0, HALF, gather, 0, unroll=32)


def make_sums(moved_rows, columns, targets, left, halves, ghosts, far):
    hbm = pl.BlockSpec(memory_space=pl.ANY)
    return pl.pallas_call(
        sums_kernel,
        grid_spec=pltpu.PrefetchScalarGridSpec(
            num_scalar_prefetch=3,
            grid=(1,),
            in_specs=[hbm] * 9,
            out_specs=[pl.BlockSpec((UCAP, B * B), lambda i, *s: (0, 0))] * 8,
            scratch_shapes=[
                pltpu.VMEM((4, ROWS + SENT, B, LANES), bf16),
                pltpu.VMEM((TABLE * HALF, LANES), bf16),
            ]
            + [pltpu.VMEM(((U_DEV + 1) * TALL, LANES), f32)] * 2
            + [
                pltpu.VMEM((SENT * ROW_LEN, LANES), bf16),
                pltpu.SemaphoreType.DMA((PARTS,)),
                pltpu.SemaphoreType.DMA((7,)),
                pltpu.SemaphoreType.DMA((3,)),
            ],
        ),
        out_shape=[jax.ShapeDtypeStruct((UCAP, B * B), bf16)] * 8,
        compiler_params=pltpu.CompilerParams(vmem_limit_bytes=VMEM_LIMIT),
        cost_estimate=pl.CostEstimate(
            flops=8_000_000_000, transcendentals=0, bytes_accessed=30_000_000
        ),
        name="sums",
    )(moved_rows, columns, targets, left, halves, *ghosts, far)


def final_kernel(
    touched, own, fine, r0, r1, r2, r3, r4, r5, g0, g1, g2, g3, g4, g5, out,
    stack, numbers, sem, number_sem,
):
    parts = (own, r0, r1, r2, r3, r4, r5, fine)
    ghosts = (g0, g1, g2, g3, g4, g5)
    copies = [
        pltpu.make_async_copy(
            ghosts[f ^ 1].at[GHOST_LEN:NEAR_AT, :], numbers.at[f], number_sem.at[f]
        )
        for f in range(6)
    ]
    copies += [
        pltpu.make_async_copy(parts[v], stack.at[v * UCAP : (v + 1) * UCAP, :], sem.at[v])
        for v in range(8)
    ]
    for copy in copies:
        copy.start()
    lane = lax.broadcasted_iota(jnp.int32, (1, LANES), 1) // UCAP
    wide = touched[...]
    for copy in copies:
        copy.wait()
    given = [numbers[f].astype(f32) for f in range(6)]
    first = wide[:, :LANES].astype(f32)
    for f in range(3):
        first = jnp.where(lane == f + 1, given[f][0:1, :], first)
    second = jnp.concatenate([wide[:, :UCAP]] * 4, axis=1).astype(f32)
    for f in range(3, 6):
        second = jnp.where(lane == f - 3, given[f][1:2, :], second)
    row = lax.broadcasted_iota(jnp.int32, (CE_DEV, LANES), 0).astype(f32)
    select = jnp.concatenate(
        [(row == first).astype(f32), (row == second).astype(f32)], axis=1
    ).astype(bf16)
    for n in range(8):
        lanes = slice(n * 4 * LANES, (n + 1) * 4 * LANES)
        out[:, lanes] = jnp.dot(select, stack[:, lanes], preferred_element_type=f32)


def make_final(touched, own, fine, got, ghosts):
    hbm = pl.BlockSpec(memory_space=pl.ANY)
    return pl.pallas_call(
        final_kernel,
        grid=(1,),
        in_specs=[pl.BlockSpec((1, U_DEV), lambda i: (0, 0))] + [hbm] * 14,
        out_specs=pl.BlockSpec((CE_DEV, B * B), lambda i: (0, 0)),
        scratch_shapes=[
            pltpu.VMEM((8 * UCAP, B * B), bf16),
            pltpu.VMEM((6, EXTRA, LANES), bf16),
            pltpu.SemaphoreType.DMA((8,)),
            pltpu.SemaphoreType.DMA((6,)),
        ],
        out_shape=jax.ShapeDtypeStruct((CE_DEV, B * B), f32),
        compiler_params=pltpu.CompilerParams(vmem_limit_bytes=VMEM_LIMIT),
        name="final",
    )(touched, own, fine, *got, *ghosts)


def neighbour_shift(value, facing):
    axis = AXES[facing // 2]
    return shifted(value, axis, 1 - 2 * (facing % 2))


def one_shard(blocks, prolong, new_owner, arrival, columns, targets, ghost_lists, touched):
    own_layer = lax.axis_index("gz")
    planes = jnp.transpose(blocks, (1, 2, 0))
    halves, *outbound, far = pack(
        own_layer[None], jnp.transpose(ghost_lists, (1, 0, 2)), new_owner[None], touched,
        prolong, planes,
    )
    ghosts = []
    for facing in range(6):
        ghosts.append(neighbour_shift(outbound[facing ^ 1], facing ^ 1))
    far_in = lax.all_to_all(
        far.reshape(LAYERS, FAR * ROW_LEN, LANES), "gz", split_axis=0, concat_axis=0, tiled=True
    )
    left = make_left(arrival[None], planes, halves)

    old = jnp.arange(ROWS, dtype=jnp.int32)
    labels = jnp.arange(LAYERS, dtype=jnp.int32)
    ranks = jnp.arange(FAR, dtype=jnp.int32)
    later = FAR + jnp.arange(NEAR, dtype=jnp.int32)
    codes = ROWS + jnp.concatenate(
        [
            (labels[:, None] * CAP + ranks[None, :]).reshape(-1),
            (own_layer - 1) * CAP + later,
            (own_layer + 1) * CAP + later,
        ]
    )
    match = (codes[:, None] == arrival[None, :]) & (codes[:, None] >= ROWS)
    row_of = jnp.sum(jnp.where(match, old[None, :] + 1, 0), axis=1) - 1
    own, fine, *sends = make_sums(
        row_of[None, :], columns.T, targets.T, left, halves, ghosts,
        far_in.reshape(LAYERS * FAR * ROW_LEN, LANES),
    )
    got = [neighbour_shift(sends[facing], facing) for facing in range(6)]
    return make_final(touched, own, fine, got, ghosts)


def solution(mesh):
    return jax.shard_map(
        one_shard,
        mesh=mesh,
        in_specs=(
            P(AXES, None, None),
            P(AXES, None),
            P(AXES),
            P(AXES),
            P(AXES, None),
            P(AXES, None),
            P(AXES, None, None),
            P(AXES, None),
        ),
        out_specs=P(AXES, None),
        check_vma=False,
    )
```
